128 devices in a mesh: ctx: 16 (over z, x), head: 8 (over y, core).
Axes of the slice: x: 4, y: 4, z: 4, core: 2. Of those that a mesh axis runs over, the one named last changes fastest.
Arguments:
- tokens: bfloat16 [32768, 2048], P('ctx'), may hold values from -6 to 6
- project_weight: bfloat16 [2048, 3, 4096], P(None, None, 'head'), may hold values from -0.125 to 0.125
- level_weight: bfloat16 [32, 128, 17], P('head'), may hold values from -0.5 to 0.5
- norm_gain: float32 [4096], P('head'), may hold values from 0.25 to 1.75
- output_weight: bfloat16 [4096, 2048], P('head'), may hold values from -0.09375 to 0.09375
Outputs:
- layer_out: bfloat16 [32768, 2048], P('ctx', 'head')
The draws below stay inside these ranges and needn't reach their ends.
All inputs are finite; a program needn't handle non-finite values.
Results may differ from the reference program's by a relative error of at most 0.015.
Values may be sent and summed in bfloat16 or wider, within the bound.
No kernel may reach another device: no remote copies, remote signals or barrier semaphores. Data moves between devices by JAX's collectives and lax.ppermute only.
A program may use at most 128 MiB of HBM per device.

```python
import jax
import jax.numpy as jnp
from jax import lax

D = 2048
H = 32
DH = 128
LEVELS = 17
TOK_DEV = 2048
TOKENS = 32768
N_CTX = 16
N_HEAD = 8


def block_levels(own_key, shape, cuts, least, top_value):
    gain = 1.0
    for axis_at, parts in cuts:
        draws = jax.random.uniform(jax.random.fold_in(jax.random.fold_in(own_key, 6), axis_at), (parts,), jnp.float32, least / len(cuts), top_value / len(cuts))
        gain = gain * jnp.repeat(jnp.exp(draws), shape[axis_at] // parts).reshape((-1,) + (1,) * (len(shape) - 1 - axis_at))
    return gain


def centred(stream_key, shape, width, most, shards=(), held_as=jnp.bfloat16):
    values = jax.random.normal(stream_key, shape, jnp.float32) * width
    if len(shards) > 0:
        values = block_levels(stream_key, shape, shards, -0.22, 0.18) * values
    return jnp.clip(values, min=-most, max=most).astype(held_as)


def setup_inputs(seed: int = 0) -> dict:
    keys = jax.random.split(jax.random.key(seed), 6)
    return {
        "tokens": centred(keys[0], (TOKENS, D), 1.0, 6.0, ((0, 16),)),
        "project_weight": centred(keys[1], (D, 3, H * DH), D ** -0.5, 0.125, ((2, 8),)),
        "level_weight": centred(keys[2], (H, DH, LEVELS), DH ** -0.5, 0.5, ((0, 8),)),
        "norm_gain": jnp.clip(1.0 + 0.15 * jax.random.normal(keys[3], (H * DH,), jnp.float32), 0.25, 1.75),
        "output_weight": centred(keys[4], (H * DH, D), (H * DH) ** -0.5, 0.09375, ((0, 8),)),
    }


def highest_bit(numbers, width_bits):
    result = jnp.zeros(numbers.shape, jnp.int32)
    for shift_count in range(width_bits):
        result = result + (jnp.right_shift(numbers, shift_count) > 0).astype(jnp.int32)
    return result

def unfold_rows(folded):
    halves = folded.reshape((N_CTX, 2, TOK_DEV // 2) + folded.shape[1:])
    ordered = jnp.concatenate([halves[:, 0], halves[::-1, 1]], axis=0)
    return ordered.reshape(folded.shape)

def fold_rows(ordered):
    pieces = ordered.reshape((2 * N_CTX, TOK_DEV // 2) + ordered.shape[1:])
    stacked = jnp.stack([pieces[:N_CTX], pieces[N_CTX:][::-1]], axis=1)
    return stacked.reshape(ordered.shape)

def reference(tokens, project_weight, level_weight, norm_gain, output_weight):
    local_bits = TOK_DEV.bit_length() - 1
    ctx_bits = N_CTX.bit_length() - 1
    width_heads = H * DH
    ordered = unfold_rows(tokens)
    projected = jnp.dot(ordered, project_weight.reshape(D, 3 * width_heads), preferred_element_type=jnp.float32).astype(jnp.bfloat16)
    projected = lax.optimization_barrier(projected).astype(jnp.float32)
    query_rows = projected[:, :width_heads].reshape(N_CTX, TOK_DEV, H, DH)
    key_rows = projected[:, width_heads:2 * width_heads].reshape(N_CTX, TOK_DEV, H, DH)
    value_rows = projected[:, 2 * width_heads:].reshape(N_CTX, TOK_DEV, H, DH)
    level_gate = jax.nn.softplus(jnp.einsum('bthd,hdl->bthl', query_rows, level_weight.astype(jnp.float32)))
    level_scale = jnp.exp2(-0.5 * jnp.arange(LEVELS, dtype=jnp.float32))
    level_coef = level_gate * level_scale
    block_state = jnp.einsum('bthd,bthe->bhde', key_rows, value_rows)
    block_ids = jnp.arange(N_CTX, dtype=jnp.int32)
    distance = highest_bit(jnp.bitwise_xor(block_ids[:, None], block_ids[None, :]), ctx_bits)
    earlier = block_ids[None, :] < block_ids[:, None]
    level_ids = jnp.arange(1, ctx_bits + 1, dtype=jnp.int32)
    selector = jnp.logical_and(earlier[:, None, :], distance[:, None, :] == level_ids[None, :, None]).astype(jnp.float32)
    far_states = jnp.einsum('bmc,chde->bmhde', selector, block_state, precision=lax.Precision.HIGHEST)
    position = jnp.arange(TOK_DEV, dtype=jnp.int32)
    level_grid = highest_bit(jnp.bitwise_xor(position[:, None], position[None, :]), local_bits)
    causal = position[None, :] <= position[:, None]

    def one_block(inputs):
        query_slab, key_slab, value_slab, coef_slab, state_slab = inputs
        scores = jnp.einsum('thd,shd->hts', query_slab, key_slab)
        weight = jnp.zeros(scores.shape, jnp.float32)
        for level_index in range(local_bits + 1):
            picked = jnp.logical_and(level_grid == level_index, causal).astype(jnp.float32)
            weight = weight + picked[None] * jnp.transpose(coef_slab[:, :, level_index])[:, :, None]
        mixed = (scores * weight).astype(jnp.bfloat16)
        mixed = lax.optimization_barrier(mixed).astype(jnp.float32)
        near = jnp.einsum('hts,she->the', mixed, value_slab)
        far_terms = jnp.einsum('thd,mhde->thme', query_slab, state_slab, precision=lax.Precision.HIGHEST)
        far_coef = coef_slab[:, :, local_bits + 1:local_bits + 1 + ctx_bits]
        combined = near + lax.optimization_barrier(jnp.sum(far_coef[..., None] * far_terms, axis=2))
        normed = combined * lax.rsqrt(lax.optimization_barrier(jnp.mean(combined * combined, axis=-1, keepdims=True)) + 1e-06) * norm_gain.reshape(H, DH)
        return normed.astype(jnp.bfloat16).reshape(TOK_DEV, H * DH)
    attended = lax.map(one_block, (query_rows, key_rows, value_rows, level_coef, far_states)).reshape(TOKENS, H * DH)
    group_width = width_heads // N_HEAD
    summed = jnp.zeros((TOKENS, D), jnp.float32)
    for group_index in range(N_HEAD):
        partial_value = jnp.dot(attended[:, group_index * group_width:(group_index + 1) * group_width], output_weight[group_index * group_width:(group_index + 1) * group_width], preferred_element_type=jnp.float32)
        summed = summed + lax.optimization_barrier(partial_value.astype(jnp.bfloat16)).astype(jnp.float32)
    return fold_rows(summed.astype(jnp.bfloat16))
```

```python
import functools

import jax
import jax.numpy as jnp
from jax import lax
from jax.experimental import pallas as pl
from jax.experimental.pallas import tpu as pltpu
from jax.sharding import PartitionSpec as P

BF16 = jnp.bfloat16
F32 = jnp.float32
CHUNK = 256
TILE = 128
LANES = 32


def dot(a, b):
    return jnp.dot(a, b, preferred_element_type=F32)


def dot_nt(a, b):
    return lax.dot_general(a, b, (((1,), (1,)), ((), ())), preferred_element_type=F32)


def dot_tn(a, b):
    return lax.dot_general(a, b, (((0,), (0,)), ((), ())), preferred_element_type=F32)


def column(coef, head, level):
    lane = head * LANES + level
    return coef[:, lane : lane + 1]


def key_value_kernel(heads, dim, tok, wk, wv, k_out, v_out, chunk_out, total_out, total):
    step = pl.program_id(0)
    rows = tok[...]
    keys = dot(rows, wk[...]).astype(BF16)
    k_out[...] = keys
    values = dot(rows, wv[...]).astype(BF16)
    v_out[...] = values

    @pl.when(step == 0)
    def _():
        total[...] = jnp.zeros_like(total)

    for head in range(heads):
        cols = slice(head * dim, (head + 1) * dim)
        state = dot_tn(keys[:, cols], values[:, cols])
        chunk_out[head] = state.astype(BF16)
        total[head] += state

    @pl.when(step == pl.num_programs(0) - 1)
    def _():
        total_out[...] = total[...].astype(BF16)


def key_value(tokens, weights, half, heads, dim):
    depth = tokens.shape[1]
    rows = tokens.shape[0] // 2
    width = heads * dim
    steps = rows // CHUNK
    return pl.pallas_call(
        functools.partial(key_value_kernel, heads, dim),
        grid=(steps,),
        in_specs=[
            pl.BlockSpec((CHUNK, depth), lambda i: (half * steps + i, 0)),
            pl.BlockSpec((None, depth, width), lambda i: (1, 0, 0)),
            pl.BlockSpec((None, depth, width), lambda i: (2, 0, 0)),
        ],
        out_specs=[
            pl.BlockSpec((CHUNK, width), lambda i: (i, 0)),
            pl.BlockSpec((CHUNK, width), lambda i: (i, 0)),
            pl.BlockSpec((None, heads, dim, dim), lambda i: (i, 0, 0, 0)),
            pl.BlockSpec((heads, dim, dim), lambda i: (0, 0, 0)),
        ],
        out_shape=[
            jax.ShapeDtypeStruct((rows, width), BF16),
            jax.ShapeDtypeStruct((rows, width), BF16),
            jax.ShapeDtypeStruct((steps, heads, dim, dim), BF16),
            jax.ShapeDtypeStruct((heads, dim, dim), BF16),
        ],
        scratch_shapes=[pltpu.VMEM((heads, dim, dim), F32)],
        cost_estimate=pl.CostEstimate(
            flops=2 * rows * depth * 2 * width, bytes_accessed=8 << 20, transcendentals=0
        ),
        name="key_value",
    )(tokens, weights, weights)


def near_kernel(heads, dim, tok, wq, k_ref, v_ref, states, gate_w, scale, near_out, q_out, coef_out):
    step = pl.program_id(0)
    queries = dot(tok[...], wq[...]).astype(BF16)
    q_out[...] = queries
    logits = dot(queries, gate_w[...])
    gate = jnp.maximum(logits, 0.0) + jnp.log1p(jnp.exp(-jnp.abs(logits)))
    coef = gate * scale[...]
    coef_out[...] = coef
    t_at = lax.broadcasted_iota(jnp.int32, (TILE, TILE), 0)
    s_at = lax.broadcasted_iota(jnp.int32, (TILE, TILE), 1)
    differ = jnp.bitwise_xor(t_at, s_at)
    odd = (step % 2).astype(F32)
    upper = (step // 2).astype(F32)
    sibling = jnp.maximum(step - 1, 0)
    for head in range(heads):
        cols = slice(head * dim, (head + 1) * dim)
        query = queries[:, cols]
        key = k_ref[:, cols]
        value = v_ref[:, cols]
        parts = []
        for tile in range(2):
            rows = slice(tile * TILE, (tile + 1) * TILE)
            part_coef = coef[rows]
            weight = jnp.broadcast_to(column(part_coef, head, 0), (TILE, TILE))
            for level in range(1, 8):
                weight = jnp.where(
                    differ >= 2 ** (level - 1), column(part_coef, head, level), weight
                )
            weight = jnp.where(t_at >= s_at, weight, 0.0)
            if tile == 1:
                far = jnp.broadcast_to(column(part_coef, head, 8), (TILE, TILE))
                weight = jnp.concatenate([far, weight], axis=1)
            score = dot_nt(query[rows], key[: (tile + 1) * TILE])
            mixed = (score * weight).astype(BF16)
            parts.append(dot(mixed, value[: (tile + 1) * TILE]))
        near = jnp.concatenate(parts, axis=0)
        pair = states[0, head].astype(F32) + states[1, head].astype(F32)
        both = jnp.concatenate([states[sibling, head], pair.astype(BF16)], axis=1)
        wide = dot(query, both)
        near = near + (odd * column(coef, head, 9)) * wide[:, :dim]
        near = near + (upper * column(coef, head, 10)) * wide[:, dim:]
        near_out[:, cols] = near


def near_part(tokens, weights, keys, values, states, gate_w, scale, half, heads, dim):
    depth = tokens.shape[1]
    rows = tokens.shape[0] // 2
    width = heads * dim
    steps = rows // CHUNK
    return pl.pallas_call(
        functools.partial(near_kernel, heads, dim),
        grid=(steps,),
        in_specs=[
            pl.BlockSpec((CHUNK, depth), lambda i: (half * steps + i, 0)),
            pl.BlockSpec((None, depth, width), lambda i: (0, 0, 0)),
            pl.BlockSpec((CHUNK, width), lambda i: (i, 0)),
            pl.BlockSpec((CHUNK, width), lambda i: (i, 0)),
            pl.BlockSpec((steps, heads, dim, dim), lambda i: (0, 0, 0, 0)),
            pl.BlockSpec((width, heads * LANES), lambda i: (0, 0)),
            pl.BlockSpec((1, heads * LANES), lambda i: (0, 0)),
        ],
        out_specs=[
            pl.BlockSpec((CHUNK, width), lambda i: (i, 0)),
            pl.BlockSpec((CHUNK, width), lambda i: (i, 0)),
            pl.BlockSpec((CHUNK, heads * LANES), lambda i: (i, 0)),
        ],
        out_shape=[
            jax.ShapeDtypeStruct((rows, width), F32),
            jax.ShapeDtypeStruct((rows, width), BF16),
            jax.ShapeDtypeStruct((rows, heads * LANES), F32),
        ],
        cost_estimate=pl.CostEstimate(
            flops=2 * rows * depth * 2 * width, bytes_accessed=8 << 20, transcendentals=0
        ),
        name="near_part",
    )(tokens, weights, keys, values, states, gate_w, scale)


def far_kernel(heads, dim, level0, flags, near, q_ref, coef_ref, gain, *refs):
    states, (out, far) = refs[:-2], refs[-2:]
    count = far.shape[2] // dim

    @pl.when(pl.program_id(0) == 0)
    def _():
        x1, x2, x3, z1, z2, z3 = (r for r in states[:6])
        for head in range(heads):
            wide = lambda r: r[head].astype(F32)
            sums = [wide(x1), wide(x2) + wide(x3), wide(z1), wide(z2) + wide(z3)]
            for level in range(4):
                on = flags[level].astype(F32)
                far[head, :, level * dim : (level + 1) * dim] = (sums[level] * on).astype(BF16)
            if count == 5:
                total = (wide(states[6]) + wide(states[7])) + (wide(states[8]) + wide(states[9]))
                far[head, :, 4 * dim :] = total.astype(BF16)

    coef = coef_ref[...]
    for head in range(heads):
        cols = slice(head * dim, (head + 1) * dim)
        terms = dot(q_ref[:, cols], far[head])
        acc = near[:, cols]
        for level in range(count):
            acc = acc + column(coef, head, level0 + level) * terms[:, level * dim : (level + 1) * dim]
        mean = jnp.mean(acc * acc, axis=-1, keepdims=True)
        out[:, cols] = (acc * lax.rsqrt(mean + 1e-06) * gain[:, cols]).astype(BF16)


def far_part(flags, near, queries, coef, gain, states, heads, dim, level0):
    rows, width = near.shape
    count = 5 if len(states) > 6 else 4
    block = CHUNK
    whole = pl.BlockSpec((heads, dim, dim), lambda i, f: (0, 0, 0))
    return pl.pallas_call(
        functools.partial(far_kernel, heads, dim, level0),
        grid_spec=pltpu.PrefetchScalarGridSpec(
            num_scalar_prefetch=1,
            grid=(rows // block,),
            in_specs=[
                pl.BlockSpec((block, width), lambda i, f: (i, 0)),
                pl.BlockSpec((block, width), lambda i, f: (i, 0)),
                pl.BlockSpec((block, heads * LANES), lambda i, f: (i, 0)),
                pl.BlockSpec((1, width), lambda i, f: (0, 0)),
            ]
            + [whole] * len(states),
            out_specs=pl.BlockSpec((block, width), lambda i, f: (i, 0)),
            scratch_shapes=[pltpu.VMEM((heads, dim, count * dim), BF16)],
        ),
        out_shape=jax.ShapeDtypeStruct((rows, width), BF16),
        cost_estimate=pl.CostEstimate(
            flops=2 * rows * dim * width * count, bytes_accessed=5 << 20, transcendentals=0
        ),
        name="far_part",
    )(flags, near, queries, coef, gain, *states)


def project_kernel(cols, own, peer, w_own, w_peer, out):
    del cols
    out[...] = (dot(own[...], w_own[...]) + dot(peer[...], w_peer[...])).astype(BF16)


def project(cols, own, peer, w_own, w_peer, feats):
    rows, width = own.shape
    count = cols.shape[0]
    return pl.pallas_call(
        project_kernel,
        grid_spec=pltpu.PrefetchScalarGridSpec(
            num_scalar_prefetch=1,
            grid=(count,),
            in_specs=[
                pl.BlockSpec((rows, width), lambda i, c: (0, 0)),
                pl.BlockSpec((rows, width), lambda i, c: (0, 0)),
                pl.BlockSpec((width, feats), lambda i, c: (0, c[i])),
                pl.BlockSpec((width, feats), lambda i, c: (0, c[i])),
            ],
            out_specs=pl.BlockSpec((None, rows, feats), lambda i, c: (i, 0, 0)),
        ),
        out_shape=jax.ShapeDtypeStruct((count, rows, feats), BF16),
        cost_estimate=pl.CostEstimate(
            flops=4 * rows * width * feats * count, bytes_accessed=4 << 20, transcendentals=0
        ),
        name="project",
    )(cols, own, peer, w_own, w_peer)


def final_kernel(*refs):
    own, up, down, out = refs[0], refs[1], refs[2], refs[-1]
    out[...] = (own[...].astype(F32) + up[...].astype(F32) + down[...].astype(F32)).astype(BF16)


def final(parts, at, up, down, base, half):
    rows, feats = up.shape
    block = rows // 2
    spec = pl.BlockSpec((block, feats), lambda i: (i, 0))
    ins = [parts, up, down]
    in_specs = [pl.BlockSpec((None, block, feats), lambda i: (at, i, 0)), spec, spec]
    alias = {}
    if base is not None:
        ins.append(base)
        in_specs.append(pl.BlockSpec(memory_space=pl.ANY))
        alias = {3: 0}
    return pl.pallas_call(
        final_kernel,
        grid=(2,),
        in_specs=in_specs,
        out_specs=pl.BlockSpec((block, feats), lambda i: (2 * half + i, 0)),
        out_shape=jax.ShapeDtypeStruct((2 * rows, feats), BF16),
        input_output_aliases=alias,
        cost_estimate=pl.CostEstimate(flops=0, bytes_accessed=2 << 20, transcendentals=0),
        name="final",
    )(*ins)


def shards(tokens, project_weight, level_weight, norm_gain, output_weight):
    heads, dim, levels = level_weight.shape
    width = heads * dim
    half_rows = tokens.shape[0] // 2
    ctx_count = lax.axis_size("ctx")
    head_count = lax.axis_size("head")
    feats = output_weight.shape[1] // head_count
    device = lax.axis_index("ctx")
    group = lax.axis_index("head")
    ring = head_count // 2
    level0 = half_rows.bit_length()

    def over_ctx(value, mask):
        return lax.ppermute(value, "ctx", [(i, i ^ mask) for i in range(ctx_count)])

    def over_core(value):
        return lax.ppermute(value, "head", [(i, i ^ 1) for i in range(head_count)])

    def over_ring(value, shift):
        return lax.ppermute(
            value, "head", [(i, (i + 2 * shift) % head_count) for i in range(head_count)]
        )

    weights = jnp.transpose(project_weight, (1, 0, 2))
    peer_weight = over_core(output_weight)
    padded = jnp.pad(level_weight, ((0, 0), (0, 0), (0, LANES - levels)))
    same = jnp.arange(heads)[:, None] == jnp.arange(heads)[None, :]
    gate_w = jnp.where(same[:, None, :, None], padded[:, :, None, :], 0).reshape(
        width, heads * LANES
    )
    lane_level = jnp.arange(heads * LANES, dtype=jnp.int32) % LANES
    scale = jnp.exp2(-0.5 * lane_level.astype(F32))[None]
    gain = norm_gain[None]

    y_at = group // 2
    core = group % 2
    target = jnp.stack([(y_at + 2) % ring, (y_at + 1) % ring, (y_at + ring - 1) % ring, y_at])
    cols = (2 * target + core).astype(jnp.int32)
    bits = jnp.stack([(device >> j) & 1 for j in range(4)]).astype(jnp.int32)

    kv = [key_value(tokens, weights, half, heads, dim) for half in range(2)]
    gathered = []
    for half in range(2):
        total = kv[half][3]
        near_x = [over_ctx(total, k) for k in (1, 2, 3)]
        group_sum = (
            total.astype(F32) + near_x[0].astype(F32) + near_x[1].astype(F32) + near_x[2].astype(F32)
        ).astype(BF16)
        near_z = [over_ctx(group_sum, 4 * k) for k in (1, 2, 3)]
        gathered.append((near_x + near_z, [group_sum] + near_z))
    near = [
        near_part(tokens, weights, *kv[half][:3], gate_w, scale, half, heads, dim)
        for half in range(2)
    ]
    result = None
    for half in range(2):
        flags = bits if half == 0 else 1 - bits
        states = gathered[half][0] + (gathered[0][1] if half == 1 else [])
        near_rows, queries, coef = near[half]
        own = far_part(flags, near_rows, queries, coef, gain, states, heads, dim, level0)
        peer = over_core(own)
        first = project(cols[:1], own, peer, output_weight, peer_weight, feats)[0]
        cut = half_rows // 2
        from_down = over_ring(first[:cut], 1)
        from_up = over_ring(first[cut:], -1)
        rest = project(cols[1:], own, peer, output_weight, peer_weight, feats)
        up_send = jnp.concatenate(
            [(rest[0, :cut].astype(F32) + from_down.astype(F32)).astype(BF16), rest[0, cut:]], axis=0
        )
        down_send = jnp.concatenate(
            [rest[1, :cut], (rest[1, cut:].astype(F32) + from_up.astype(F32)).astype(BF16)], axis=0
        )
        arrived_up = over_ring(up_send, 1)
        arrived_down = over_ring(down_send, -1)
        result = final(rest, 2, arrived_up, arrived_down, result, half)
    return result


def solution(mesh):
    placed = (
        P("ctx", None),
        P(None, None, "head"),
        P("head", None, None),
        P("head"),
        P("head", None),
    )
    return jax.shard_map(
        shards, mesh=mesh, in_specs=placed, out_specs=P("ctx", "head"), check_vma=False
    )
```

```python
import functools

import jax
import jax.numpy as jnp
from jax import lax
from jax.experimental import pallas as pl
from jax.experimental.pallas import tpu as pltpu
from jax.sharding import PartitionSpec as P

BF16 = jnp.bfloat16
F32 = jnp.float32
BLOCK = 512
CHUNK = 256
TILE = 128
STRIDE = 24


def dot(a, b):
    return jnp.dot(a, b, preferred_element_type=F32)


def dot_nt(a, b):
    return lax.dot_general(a, b, (((1,), (1,)), ((), ())), preferred_element_type=F32)


def cost(flops, mib):
    return pl.CostEstimate(flops=flops, bytes_accessed=mib << 20, transcendentals=0)


def bits_of(number):
    return sum((number >= 2**j).astype(jnp.int32) for j in range(4))


def key_value_kernel(heads, dim, tok, wk, wv, k_out, vt_out, chunk_out, total_out, total):
    step = pl.program_id(0)
    rows = tok[...]
    keys = dot(rows, wk[...]).astype(BF16)
    k_out[...] = keys
    values = dot(rows, wv[...]).astype(BF16)

    @pl.when(step % 2 == 0)
    def _():
        total[...] = jnp.zeros_like(total)

    for head in range(heads):
        cols = slice(head * dim, (head + 1) * dim)
        turned = values[:, cols].T
        vt_out[cols] = turned
        for chunk in range(2):
            at = slice(chunk * CHUNK, (chunk + 1) * CHUNK)
            state = dot(turned[:, at], keys[at, cols])
            chunk_out[chunk, head] = state.astype(BF16)
            total[head] += state

    @pl.when(step % 2 == 1)
    def _():
        total_out[...] = total[...].astype(BF16)


def key_value(tokens, weights, heads, dim):
    rows, depth = tokens.shape
    width = heads * dim
    return pl.pallas_call(
        functools.partial(key_value_kernel, heads, dim),
        grid=(rows // BLOCK,),
        in_specs=[
            pl.BlockSpec((BLOCK, depth), lambda i: (i, 0)),
            pl.BlockSpec((None, depth, width), lambda i: (1, 0, 0)),
            pl.BlockSpec((None, depth, width), lambda i: (2, 0, 0)),
        ],
        out_specs=[
            pl.BlockSpec((BLOCK, width), lambda i: (i, 0)),
            pl.BlockSpec((width, BLOCK), lambda i: (0, i)),
            pl.BlockSpec((2, heads, dim, dim), lambda i: (i, 0, 0, 0)),
            pl.BlockSpec((None, heads, dim, dim), lambda i: (i // 2, 0, 0, 0)),
        ],
        out_shape=[
            jax.ShapeDtypeStruct((rows, width), BF16),
            jax.ShapeDtypeStruct((width, rows), BF16),
            jax.ShapeDtypeStruct((rows // CHUNK, heads, dim, dim), BF16),
            jax.ShapeDtypeStruct((2, heads, dim, dim), BF16),
        ],
        scratch_shapes=[pltpu.VMEM((heads, dim, dim), F32)],
        cost_estimate=cost(4 * rows * depth * width, 14),
        name="key_value",
    )(tokens, weights, weights)


def near_kernel(heads, dim, tok, wq, k_ref, vt_ref, states, gate_w, near_out, q_out, coef_out, steps_ref):
    step = pl.program_id(0)
    queries = dot(tok[...], wq[...]).astype(BF16)
    q_out[...] = queries
    logits = dot_nt(gate_w[...], queries)
    gate = jnp.maximum(logits, 0.0) + jnp.log1p(jnp.exp(-jnp.abs(logits)))
    level_at = lax.broadcasted_iota(jnp.int32, logits.shape, 0) % STRIDE
    coef_out[...] = gate * jnp.exp2(-0.5 * level_at.astype(F32))

    def row(head, level, count, at=slice(None)):
        return coef_out[pl.ds(head * STRIDE + level, count, stride=0), :][:, at]

    lane = lax.broadcasted_iota(jnp.int32, (16, BLOCK), 1)
    group = lax.broadcasted_iota(jnp.int32, (16, BLOCK), 0)
    query_group = jnp.bitwise_and(lane, TILE - 1) // 8
    apart = bits_of(jnp.bitwise_xor(query_group, group))
    before = query_group > group
    lane8 = jnp.bitwise_and(lane[:8], 7)
    key8 = group[:8]
    near8 = bits_of(jnp.bitwise_xor(lane8, key8))
    causal8 = lane8 >= key8
    tile_group = jnp.bitwise_and(lax.broadcasted_iota(jnp.int32, (8, CHUNK), 1), TILE - 1) // 8
    upper = (step % 2).astype(F32)
    for head in range(heads):
        cols = slice(head * dim, (head + 1) * dim)
        rough = jnp.zeros((16, BLOCK), F32)
        for level in range(1, 5):
            rough = jnp.where(apart == level, row(head, level + 3, 16), rough)
        steps_ref[...] = jnp.where(before, rough, 0.0)
        fine = row(head, 0, 8)
        for level in range(1, 4):
            fine = jnp.where(near8 == level, row(head, level, 8), fine)
        fine = jnp.where(causal8, fine, 0.0)
        pair = (states[0, head].astype(F32) + states[1, head].astype(F32)).astype(BF16)
        for chunk in range(2):
            at = slice(chunk * CHUNK, (chunk + 1) * CHUNK)
            query = queries[at, cols]
            left = [k_ref[at, cols], pair]
            if chunk == 1:
                left.append(jnp.where(step % 2 == 0, states[0, head], states[2, head]))
            score = dot_nt(jnp.concatenate(left, axis=0), query)
            top, bottom = [], []
            across = row(head, 8, 8, slice(chunk * CHUNK + TILE, (chunk + 1) * CHUNK))
            for j in range(16):
                weight = jnp.where(
                    tile_group == j, fine[:, at], steps_ref[pl.ds(j, 8, stride=0), :][:, at]
                )
                low = score[8 * j : 8 * j + 8]
                high = score[TILE + 8 * j : TILE + 8 * j + 8, TILE:]
                top.append(
                    jnp.concatenate([low[:, :TILE] * weight[:, :TILE], low[:, TILE:] * across], axis=1)
                )
                bottom.append(
                    jnp.concatenate([jnp.zeros((8, TILE), F32), high * weight[:, TILE:]], axis=1)
                )
            mixed = jnp.concatenate(top + bottom, axis=0).astype(BF16)
            near = dot(vt_ref[cols, at], mixed)
            scale = jnp.concatenate([upper * row(head, 10, 8, at)] * (dim // 8), axis=0)
            near = near + scale * score[CHUNK : CHUNK + dim]
            if chunk == 1:
                scale = jnp.concatenate([row(head, 9, 8, at)] * (dim // 8), axis=0)
                near = near + scale * score[CHUNK + dim :]
            near_out[cols, at] = near


def near_part(tokens, weights, keys, values, states, gate_w, heads, dim):
    rows, depth = tokens.shape
    width = heads * dim
    return pl.pallas_call(
        functools.partial(near_kernel, heads, dim),
        grid=(rows // BLOCK,),
        in_specs=[
            pl.BlockSpec((BLOCK, depth), lambda i: (i, 0)),
            pl.BlockSpec((None, depth, width), lambda i: (0, 0, 0)),
            pl.BlockSpec((BLOCK, width), lambda i: (i, 0)),
            pl.BlockSpec((width, BLOCK), lambda i: (0, i)),
            pl.BlockSpec((rows // 2 // CHUNK, heads, dim, dim), lambda i: (i // 2, 0, 0, 0)),
            pl.BlockSpec((heads * STRIDE, width), lambda i: (0, 0)),
        ],
        out_specs=[
            pl.BlockSpec((width, BLOCK), lambda i: (0, i)),
            pl.BlockSpec((BLOCK, width), lambda i: (i, 0)),
            pl.BlockSpec((heads * STRIDE, BLOCK), lambda i: (0, i)),
        ],
        out_shape=[
            jax.ShapeDtypeStruct((width, rows), F32),
            jax.ShapeDtypeStruct((rows, width), BF16),
            jax.ShapeDtypeStruct((heads * STRIDE, rows), F32),
        ],
        scratch_shapes=[pltpu.VMEM((16, BLOCK), F32)],
        cost_estimate=cost(4 * rows * depth * width, 14),
        name="near_part",
    )(tokens, weights, keys, values, states, gate_w)


def far_kernel(heads, dim, level0, flags, near, q_ref, coef_ref, gain, *refs):
    states, (out, far, gains) = refs[:-3], refs[-3:]
    count = far.shape[1] // dim

    @pl.when(pl.program_id(0) == 0)
    def _():
        x1, x2, x3, z1, z2, z3 = states[:6]
        for head in range(heads):
            cols = slice(head * dim, (head + 1) * dim)
            wide = lambda r: r[head].astype(F32)
            sums = [wide(x1), wide(x2) + wide(x3), wide(z1), wide(z2) + wide(z3)]
            for level in range(4):
                on = flags[level].astype(F32)
                far[head, level * dim : (level + 1) * dim] = (sums[level] * on).astype(BF16)
            if count == 5:
                total = (wide(states[6]) + wide(states[7])) + (wide(states[8]) + wide(states[9]))
                far[head, 4 * dim :] = total.astype(BF16)
            gains[cols] = jnp.broadcast_to(gain[:, cols], (dim, dim)).T

    for head in range(heads):
        cols = slice(head * dim, (head + 1) * dim)
        for chunk in range(2):
            at = slice(chunk * CHUNK, (chunk + 1) * CHUNK)
            terms = dot_nt(far[head], q_ref[at, cols])
            acc = near[cols, at]
            for level in range(count):
                scale = coef_ref[pl.ds(head * STRIDE + level0 + level, 8, stride=0), :][:, at]
                scale = jnp.concatenate([scale] * (dim // 8), axis=0)
                acc = acc + scale * terms[level * dim : (level + 1) * dim]
            mean = jnp.mean(acc * acc, axis=0, keepdims=True)
            both = jnp.concatenate([gains[cols], gains[cols]], axis=1)
            out[at, cols] = (acc * lax.rsqrt(mean + 1e-06) * both).astype(BF16).T


def far_part(flags, near, queries, coef, gain, over_x, over_z, sums, half, heads, dim, level0):
    width, rows = near.shape
    steps = rows // 2 // BLOCK
    count = 4 + half

    def whole(at):
        return pl.BlockSpec((None, heads, dim, dim), lambda i, f: (at, 0, 0, 0))

    states = over_x + over_z
    specs = [whole(half)] * len(states)
    if half == 1:
        states = states + sums
        specs = specs + [whole(0)] * len(sums)
    return pl.pallas_call(
        functools.partial(far_kernel, heads, dim, level0),
        grid_spec=pltpu.PrefetchScalarGridSpec(
            num_scalar_prefetch=1,
            grid=(steps,),
            in_specs=[
                pl.BlockSpec((width, BLOCK), lambda i, f: (0, half * steps + i)),
                pl.BlockSpec((BLOCK, width), lambda i, f: (half * steps + i, 0)),
                pl.BlockSpec((heads * STRIDE, BLOCK), lambda i, f: (0, half * steps + i)),
                pl.BlockSpec((1, width), lambda i, f: (0, 0)),
            ]
            + specs,
            out_specs=pl.BlockSpec((BLOCK, width), lambda i, f: (i, 0)),
            scratch_shapes=[
                pltpu.VMEM((heads, count * dim, dim), BF16),
                pltpu.VMEM((width, dim), F32),
            ],
        ),
        out_shape=jax.ShapeDtypeStruct((rows // 2, width), BF16),
        cost_estimate=cost(rows * dim * width * count, 5),
        name="far_part",
    )(flags, near, queries, coef, gain, *states)


def farthest_kernel(cols, own, peer, w_own, w_peer, top, bottom):
    del cols
    step = pl.program_id(0)
    result = (dot(own[...], w_own[...]) + dot(peer[...], w_peer[...])).astype(BF16)

    @pl.when(step == 0)
    def _():
        top[...] = result

    @pl.when(step == 1)
    def _():
        bottom[...] = result


def relay_kernel(cols, own, peer, up_own, up_peer, down_own, down_peer, top, bottom, up, down):
    del cols
    step = pl.program_id(0)
    mine, other = own[...], peer[...]
    upward = dot(mine, up_own[...]) + dot(other, up_peer[...])
    downward = dot(mine, down_own[...]) + dot(other, down_peer[...])

    @pl.when(step == 0)
    def _():
        up[...] = (upward + top[...].astype(F32)).astype(BF16)
        down[...] = downward.astype(BF16)

    @pl.when(step == 1)
    def _():
        up[...] = upward.astype(BF16)
        down[...] = (downward + bottom[...].astype(F32)).astype(BF16)


def final_kernel(cols, own, peer, w_own, w_peer, up, down, *refs):
    del cols
    total = dot(own[...], w_own[...]) + dot(peer[...], w_peer[...])
    refs[-1][...] = (total + up[...].astype(F32) + down[...].astype(F32)).astype(BF16)


def project(kernel, cols, targets, own, peer, weights, extra, extra_specs, out_specs, out_shape, alias, name):
    rows, width = own.shape
    block = rows // 2
    feats = 256

    def weight_at(target):
        return pl.BlockSpec((width, feats), lambda i, c: (0, c[target]))

    rowwise = pl.BlockSpec((block, width), lambda i, c: (i, 0))
    args = [own, peer]
    in_specs = [rowwise, rowwise]
    for target in targets:
        args += list(weights)
        in_specs += [weight_at(target), weight_at(target)]
    return pl.pallas_call(
        kernel,
        grid_spec=pltpu.PrefetchScalarGridSpec(
            num_scalar_prefetch=1,
            grid=(2,),
            in_specs=in_specs + extra_specs,
            out_specs=out_specs,
        ),
        out_shape=out_shape,
        input_output_aliases=alias,
        cost_estimate=cost(4 * rows * width * feats * len(targets), 4),
        name=name,
    )(cols, *args, *extra)


def shards(tokens, project_weight, level_weight, norm_gain, output_weight):
    heads, dim, levels = level_weight.shape
    width = heads * dim
    half_rows = tokens.shape[0] // 2
    quarter = half_rows // 2
    ctx_count = lax.axis_size("ctx")
    head_count = lax.axis_size("head")
    feats = output_weight.shape[1] // head_count
    device = lax.axis_index("ctx")
    group = lax.axis_index("head")
    ring = head_count // 2
    level0 = half_rows.bit_length()

    def over_ctx(value, mask):
        return lax.ppermute(value, "ctx", [(i, i ^ mask) for i in range(ctx_count)])

    def over_core(value):
        return lax.ppermute(value, "head", [(i, i ^ 1) for i in range(head_count)])

    def over_ring(value, shift):
        return lax.ppermute(
            value, "head", [(i, (i + 2 * shift) % head_count) for i in range(head_count)]
        )

    weights = jnp.transpose(project_weight, (1, 0, 2))
    peer_weight = over_core(output_weight)
    padded = jnp.pad(jnp.transpose(level_weight, (0, 2, 1)), ((0, 0), (0, STRIDE - levels), (0, 0)))
    same = jnp.arange(heads)[:, None] == jnp.arange(heads)[None, :]
    gate_w = jnp.where(same[:, None, :, None], padded[:, :, None, :], 0).reshape(
        heads * STRIDE, width
    )
    gain = norm_gain[None]
    y_at = group // 2
    core = group % 2
    target = jnp.stack([(y_at + 2) % ring, (y_at + 1) % ring, (y_at + ring - 1) % ring, y_at])
    cols = (2 * target + core).astype(jnp.int32)
    bits = jnp.stack([(device >> j) & 1 for j in range(4)]).astype(jnp.int32)

    keys, values, states, totals = key_value(tokens, weights, heads, dim)
    over_x = [over_ctx(totals, k) for k in (1, 2, 3)]
    sums = (
        totals.astype(F32) + over_x[0].astype(F32) + over_x[1].astype(F32) + over_x[2].astype(F32)
    ).astype(BF16)
    over_z = [over_ctx(sums, 4 * k) for k in (1, 2, 3)]
    near, queries, coef = near_part(tokens, weights, keys, values, states, gate_w, heads, dim)
    piece = jax.ShapeDtypeStruct((quarter, feats), BF16)
    full = jax.ShapeDtypeStruct((half_rows, feats), BF16)
    fixed = pl.BlockSpec((quarter, feats), lambda i, c: (0, 0))
    moving = pl.BlockSpec((quarter, feats), lambda i, c: (i, 0))
    result = None
    for half in range(2):
        flags = bits if half == 0 else 1 - bits
        own = far_part(
            flags, near, queries, coef, gain, over_x, over_z, [sums] + over_z, half, heads, dim, level0
        )
        peer = over_core(own)
        pair = (output_weight, peer_weight)
        top, bottom = project(
            farthest_kernel, cols, (0,), own, peer, pair, [], [], [fixed, fixed], [piece, piece], {}, "farthest"
        )
        from_down = over_ring(top, 1)
        from_up = over_ring(bottom, -1)
        up, down = project(
            relay_kernel, cols, (1, 2), own, peer, pair, [from_down, from_up], [fixed, fixed],
            [moving, moving], [full, full], {}, "relay",
        )
        arrived_up = over_ring(up, 1)
        arrived_down = over_ring(down, -1)
        extra, specs, alias = [arrived_up, arrived_down], [moving, moving], {}
        if half == 1:
            extra.append(result)
            specs = specs + [pl.BlockSpec(memory_space=pl.ANY)]
            alias = {7: 0}
        result = project(
            final_kernel, cols, (3,), own, peer, pair, extra, specs,
            pl.BlockSpec((quarter, feats), functools.partial(lambda h, i, c: (2 * h + i, 0), half)),
            jax.ShapeDtypeStruct((2 * half_rows, feats), BF16), alias, "final",
        )
    return result


def solution(mesh):
    placed = (
        P("ctx", None),
        P(None, None, "head"),
        P("head", None, None),
        P("head"),
        P("head", None),
    )
    return jax.shard_map(
        shards, mesh=mesh, in_specs=placed, out_specs=P("ctx", "head"), check_vma=False
    )
```

```python
import functools

import jax
import jax.numpy as jnp
from jax import lax
from jax.experimental import pallas as pl
from jax.experimental.pallas import tpu as pltpu
from jax.sharding import PartitionSpec as P

BF16 = jnp.bfloat16
F32 = jnp.float32
BLOCK = 512
CHUNK = 256
TILE = 128
KV = 28
SMALL = 4


def dot(a, b):
    return jnp.dot(a, b, preferred_element_type=F32)


def dot_nt(a, b):
    return lax.dot_general(a, b, (((1,), (1,)), ((), ())), preferred_element_type=F32)


def cost(flops, mib):
    return pl.CostEstimate(flops=flops, bytes_accessed=mib << 20, transcendentals=0)


def bits_of(number):
    return sum((number >= 2**j).astype(jnp.int32) for j in range(4))


def key_value_block(heads, dim, block, rows, wk, wv, k_out, vt_out, chunk_out, total, keys=None):
    at = slice(block * BLOCK, (block + 1) * BLOCK)
    if keys is None:
        keys = dot(rows, wk[...])
    keys = keys.astype(BF16)
    k_out[at] = keys
    values = dot(rows, wv[...]).astype(BF16)
    for head in range(heads):
        cols = slice(head * dim, (head + 1) * dim)
        turned = values[:, cols].T
        vt_out[block, cols] = turned
        sums = None if block == 0 else total[head]
        for chunk in range(2):
            inner = slice(chunk * CHUNK, (chunk + 1) * CHUNK)
            state = dot(turned[:, inner], keys[inner, cols])
            chunk_out[2 * block + chunk, head] = state.astype(BF16)
            sums = state if sums is None else sums + state
        total[head] = sums


def first_kernel(heads, dim, tok_in, w_in, k_out, vt_out, chunk_out, total_out, tok, wq, wk, wv, total, sems):
    depth = tok.shape[1]
    part = depth // 2
    blocks = k_out.shape[0] // BLOCK
    head_rows = pl.ds(0, BLOCK)
    pairs = []
    for j in range(2):
        at = pl.ds(j * part, part)
        pairs.append((w_in.at[1, at], wk.at[at]))
        pairs.append((tok_in.at[head_rows, at], tok.at[head_rows, at]))
    pairs.append((w_in.at[2], wv))
    rest = pl.ds(BLOCK, tok.shape[0] - BLOCK)
    pairs.append((tok_in.at[rest], tok.at[rest]))
    pairs.append((w_in.at[0], wq))
    copies = [pltpu.make_async_copy(*pair, sems.at[j]) for j, pair in enumerate(pairs)]
    for copy in copies[:4]:
        copy.start()
    keys = None
    for j in range(2):
        copies[2 * j].wait()
        copies[2 * j + 1].wait()
        for copy in copies[4 + j : 5 + 2 * j]:
            copy.start()
        at = slice(j * part, (j + 1) * part)
        term = dot(tok[:BLOCK, at], wk[at])
        keys = term if keys is None else keys + term
    copies[4].wait()
    outs = (wk, wv, k_out, vt_out, chunk_out, total)
    key_value_block(heads, dim, 0, tok[:BLOCK], *outs, keys)
    copies[5].wait()
    for block in range(1, blocks):
        key_value_block(heads, dim, block, tok[block * BLOCK : (block + 1) * BLOCK], *outs)
    copies[6].wait()
    total_out[...] = total[...].astype(BF16)


def second_kernel(heads, dim, tok, wk, wv, k_out, vt_out, chunk_out, total_out, total):
    half = tok.shape[0] // 2
    for block in range(half // BLOCK):
        at = slice(half + block * BLOCK, half + (block + 1) * BLOCK)
        key_value_block(heads, dim, block, tok[at], wk, wv, k_out, vt_out, chunk_out, total)
    total_out[...] = total[...].astype(BF16)


def key_value(heads, dim, rows, args, first):
    depth = args[0].shape[1]
    width = heads * dim
    vmem = pl.BlockSpec(memory_space=pltpu.VMEM)
    shapes = [
        jax.ShapeDtypeStruct((rows, width), BF16),
        jax.ShapeDtypeStruct((rows // BLOCK, width, BLOCK), BF16),
        jax.ShapeDtypeStruct((rows // CHUNK, heads, dim, dim), BF16),
        jax.ShapeDtypeStruct((heads, dim, dim), BF16),
    ]
    scratch = [pltpu.VMEM((heads, dim, dim), F32)]
    if first:
        shapes.append(jax.ShapeDtypeStruct(args[0].shape, BF16))
        shapes += [jax.ShapeDtypeStruct((depth, width), BF16)] * 3
        scratch.append(pltpu.SemaphoreType.DMA((7,)))
    return pl.pallas_call(
        functools.partial(first_kernel if first else second_kernel, heads, dim),
        in_specs=[pl.BlockSpec(memory_space=pltpu.HBM)] * 2 if first else [vmem] * 3,
        out_specs=[vmem] * len(shapes),
        out_shape=shapes,
        scratch_shapes=scratch,
        compiler_params=pltpu.CompilerParams(vmem_limit_bytes=(KV if first else SMALL) << 20),
        cost_estimate=cost(4 * rows * depth * width, 14),
        name="key_value",
    )(*args)


def sums_kernel(*refs):
    count = len(refs) // 3
    for j in range(count):
        refs[2 * count + j][...] = (refs[2 * j][...].astype(F32) + refs[2 * j + 1][...].astype(F32)).astype(BF16)


def added(*pairs):
    vmem = pl.BlockSpec(memory_space=pltpu.VMEM)
    flat = [value for pair in pairs for value in pair]
    return pl.pallas_call(
        sums_kernel,
        in_specs=[vmem] * len(flat),
        out_specs=[vmem] * len(pairs),
        out_shape=[jax.ShapeDtypeStruct(pair[0].shape, BF16) for pair in pairs],
        compiler_params=pltpu.CompilerParams(vmem_limit_bytes=SMALL << 20),
        cost_estimate=cost(1 << 18, 1),
        name="added",
    )(*flat)


def near_kernel(
    heads, dim, half, step, tok, wq, keys, vt, states, level_w, after, near_out, q_out, coef_out, steps_ref
):
    del after
    first = half * (tok.shape[0] // 2) + step * BLOCK
    k_ref = keys.at[pl.ds(step * BLOCK, BLOCK)]
    vt_ref = vt.at[step]
    queries = dot(tok[first : first + BLOCK], wq[...]).astype(BF16)
    q_out[...] = queries
    levels = level_w.shape[0]
    count = levels * heads
    flat = level_w[...].astype(F32).reshape(count, dim)
    owner = lax.broadcasted_iota(jnp.int32, (count, heads * dim), 0) % heads
    lane_head = lax.broadcasted_iota(jnp.int32, (count, heads * dim), 1) // dim
    gate_w = jnp.where(owner == lane_head, jnp.concatenate([flat] * heads, axis=1), 0.0)
    logits = dot_nt(gate_w.astype(BF16), queries)
    gate = jnp.maximum(logits, 0.0) + jnp.log1p(jnp.exp(-jnp.abs(logits)))
    level_at = lax.broadcasted_iota(jnp.int32, logits.shape, 0) // heads
    coef_out[...] = gate * jnp.exp2(-0.5 * level_at.astype(F32))

    def row(head, level, count, at=slice(None)):
        return coef_out[pl.ds(level * heads + head, count, stride=0), :][:, at]

    lane = lax.broadcasted_iota(jnp.int32, (16, BLOCK), 1)
    group = lax.broadcasted_iota(jnp.int32, (16, BLOCK), 0)
    query_group = jnp.bitwise_and(lane, TILE - 1) // 8
    apart = bits_of(jnp.bitwise_xor(query_group, group))
    before = query_group > group
    lane8 = jnp.bitwise_and(lane[:8], 7)
    key8 = group[:8]
    near8 = bits_of(jnp.bitwise_xor(lane8, key8))
    causal8 = lane8 >= key8
    tile_group = jnp.bitwise_and(lax.broadcasted_iota(jnp.int32, (8, CHUNK), 1), TILE - 1) // 8
    for head in range(heads):
        cols = slice(head * dim, (head + 1) * dim)
        rough = jnp.zeros((16, BLOCK), F32)
        for level in range(1, 5):
            rough = jnp.where(apart == level, row(head, level + 3, 16), rough)
        steps_ref[...] = jnp.where(before, rough, 0.0)
        fine = row(head, 0, 8)
        for level in range(1, 4):
            fine = jnp.where(near8 == level, row(head, level, 8), fine)
        fine = jnp.where(causal8, fine, 0.0)
        pair = (states[0, head].astype(F32) + states[1, head].astype(F32)).astype(BF16)
        for chunk in range(2):
            at = slice(chunk * CHUNK, (chunk + 1) * CHUNK)
            query = queries[at, cols]
            left = [k_ref[at, cols]]
            if step == 1:
                left.append(pair)
            if chunk == 1:
                left.append(states[2 * step, head])
            score = dot_nt(jnp.concatenate(left, axis=0), query)
            top, bottom = [], []
            across = row(head, 8, 8, slice(chunk * CHUNK + TILE, (chunk + 1) * CHUNK))
            for j in range(16):
                weight = jnp.where(
                    tile_group == j, fine[:, at], steps_ref[pl.ds(j, 8, stride=0), :][:, at]
                )
                low = score[8 * j : 8 * j + 8]
                high = score[TILE + 8 * j : TILE + 8 * j + 8, TILE:]
                top.append(
                    jnp.concatenate([low[:, :TILE] * weight[:, :TILE], low[:, TILE:] * across], axis=1)
                )
                bottom.append(
                    jnp.concatenate([jnp.zeros((8, TILE), F32), high * weight[:, TILE:]], axis=1)
                )
            mixed = jnp.concatenate(top + bottom, axis=0).astype(BF16)
            near = dot(vt_ref[cols, at], mixed)
            wider = ([10] if step == 1 else []) + ([9] if chunk == 1 else [])
            for order, level in enumerate(wider):
                scale = jnp.concatenate([row(head, level, 8, at)] * (dim // 8), axis=0)
                near = near + scale * score[CHUNK + order * dim : CHUNK + (order + 1) * dim]
            near_out[cols, at] = near


def near_part(held, after, half, step, heads, dim):
    depth = held[0].shape[1]
    width = heads * dim
    vmem = pl.BlockSpec(memory_space=pltpu.VMEM)
    return pl.pallas_call(
        functools.partial(near_kernel, heads, dim, half, step),
        in_specs=[vmem] * 6 + [pl.BlockSpec(memory_space=pl.ANY)],
        out_specs=[vmem] * 3,
        out_shape=[
            jax.ShapeDtypeStruct((width, BLOCK), F32),
            jax.ShapeDtypeStruct((BLOCK, width), BF16),
            jax.ShapeDtypeStruct((held[5].shape[0] * heads, BLOCK), F32),
        ],
        scratch_shapes=[pltpu.VMEM((16, BLOCK), F32)],
        compiler_params=pltpu.CompilerParams(vmem_limit_bytes=SMALL << 20),
        cost_estimate=cost(4 * BLOCK * depth * width, 14),
        name="near_part",
    )(*held, after)


def far_kernel(heads, dim, level0, count, half, device, after, gain, *refs):
    del after
    bits = [(device[0] >> level) & 1 for level in range(4)]
    flags = [(bit if half == 0 else 1 - bit).astype(F32) for bit in bits]
    blocks = (len(refs) - count - 2) // 3
    states, (out, gains) = refs[3 * blocks : -2], refs[-2:]
    for head in range(heads):
        cols = slice(head * dim, (head + 1) * dim)
        gains[cols] = jnp.broadcast_to(gain[:, cols], (dim, dim)).T
    for block in range(blocks):
        near, q_ref, coef_ref = refs[3 * block : 3 * block + 3]
        for head in range(heads):
            cols = slice(head * dim, (head + 1) * dim)
            far = jnp.concatenate([state[head] for state in states], axis=0)
            for chunk in range(2):
                at = slice(chunk * CHUNK, (chunk + 1) * CHUNK)
                terms = dot_nt(far, q_ref[at, cols])
                acc = near[cols, at]
                for level in range(count):
                    lane = (level0 + level) * heads + head
                    scale = coef_ref[pl.ds(lane, 8, stride=0), :][:, at]
                    if level < 4:
                        scale = scale * flags[level]
                    scale = jnp.concatenate([scale] * (dim // 8), axis=0)
                    acc = acc + scale * terms[level * dim : (level + 1) * dim]
                mean = jnp.mean(acc * acc, axis=0, keepdims=True)
                both = jnp.concatenate([gains[cols], gains[cols]], axis=1)
                rows = slice(block * BLOCK + chunk * CHUNK, block * BLOCK + (chunk + 1) * CHUNK)
                out[rows, cols] = (acc * lax.rsqrt(mean + 1e-06) * both).astype(BF16).T


def far_part(device, after, near, gain, states, heads, dim, level0):
    rows = len(near) * BLOCK
    width = heads * dim
    count = len(states)
    blocks = [part for block in near for part in block]
    vmem = pl.BlockSpec(memory_space=pltpu.VMEM)
    return pl.pallas_call(
        functools.partial(far_kernel, heads, dim, level0, count, count - 4),
        in_specs=[pl.BlockSpec(memory_space=pltpu.SMEM), pl.BlockSpec(memory_space=pl.ANY)]
        + [vmem] * (1 + len(blocks) + count),
        out_specs=vmem,
        out_shape=jax.ShapeDtypeStruct((rows, width), BF16),
        scratch_shapes=[pltpu.VMEM((width, dim), F32)],
        compiler_params=pltpu.CompilerParams(vmem_limit_bytes=SMALL << 20),
        cost_estimate=cost(2 * rows * dim * width * count, 5),
        name="far_part",
    )(device, after, gain, *blocks, *states)


def project_kernel(feats, ring, group, own, peer, w_own, w_peer, top, bottom, up, down, mine):
    block = own.shape[0] // 2
    for order, shift in enumerate((2, 1, ring - 1, 0)):
        slot = 2 * (((group[0] >> 1) + shift) % ring) + (group[0] & 1)
        at = pl.ds(pl.multiple_of(slot * feats, feats), feats)
        for part in range(2):
            rows = slice(part * block, (part + 1) * block)
            total = dot(own[rows], w_own[:, at]) + dot(peer[rows], w_peer[:, at])
            if order == 0:
                (top, bottom)[part][...] = total.astype(BF16)
            else:
                out = (up, down, mine)[order - 1]
                out[rows] = total.astype(out.dtype)


def project(group, ring, own, peer, w_own, w_peer, feats):
    rows, width = own.shape
    vmem = pl.BlockSpec(memory_space=pltpu.VMEM)
    return pl.pallas_call(
        functools.partial(project_kernel, feats, ring),
        in_specs=[pl.BlockSpec(memory_space=pltpu.SMEM)] + [vmem] * 4,
        out_specs=[vmem] * 5,
        out_shape=[jax.ShapeDtypeStruct((rows // 2, feats), BF16)] * 2
        + [jax.ShapeDtypeStruct((rows, feats), BF16)] * 2
        + [jax.ShapeDtypeStruct((rows, feats), F32)],
        compiler_params=pltpu.CompilerParams(vmem_limit_bytes=12 << 20),
        cost_estimate=cost(16 * rows * width * feats, 4),
        name="project",
    )(group, own, peer, w_own, w_peer)


def relay_kernel(up_in, down_in, from_down, from_up, after, up, down):
    del after
    block = from_down.shape[0]
    up[:block] = (up_in[:block].astype(F32) + from_down[...].astype(F32)).astype(BF16)
    up[block:] = up_in[block:]
    down[:block] = down_in[:block]
    down[block:] = (down_in[block:].astype(F32) + from_up[...].astype(F32)).astype(BF16)


def relay(up, down, from_down, from_up, after):
    vmem = pl.BlockSpec(memory_space=pltpu.VMEM)
    return pl.pallas_call(
        relay_kernel,
        in_specs=[vmem] * 4 + [pl.BlockSpec(memory_space=pl.ANY)],
        out_specs=[vmem] * 2,
        out_shape=[jax.ShapeDtypeStruct(up.shape, BF16)] * 2,
        compiler_params=pltpu.CompilerParams(vmem_limit_bytes=SMALL << 20),
        cost_estimate=cost(1 << 18, 1),
        name="relay",
    )(up, down, from_down, from_up, after)


def shards(tokens, project_weight, level_weight, norm_gain, output_weight):
    heads, dim, _ = level_weight.shape
    half_rows = tokens.shape[0] // 2
    ctx_count = lax.axis_size("ctx")
    head_count = lax.axis_size("head")
    feats = output_weight.shape[1] // head_count
    device = lax.axis_index("ctx")
    group = lax.axis_index("head")
    ring = head_count // 2
    level0 = half_rows.bit_length()

    def over_core(value):
        return lax.ppermute(value, "head", [(i, i ^ 1) for i in range(head_count)])

    def over_ring(value, shift):
        return lax.ppermute(
            value, "head", [(i, (i + 2 * shift) % head_count) for i in range(head_count)]
        )

    weights = jnp.transpose(project_weight, (1, 0, 2))
    peer_weight = over_core(output_weight)
    gate_w = jnp.transpose(level_weight, (2, 0, 1))
    gain = norm_gain[None]
    tokens, where_ctx, where_head = lax.optimization_barrier(
        (tokens, device.reshape(1), group.reshape(1))
    )

    def over_ctx(value, mask):
        return lax.ppermute(value, "ctx", [(i, i ^ mask) for i in range(ctx_count)])

    low = key_value(heads, dim, half_rows, (tokens, weights), True)
    rows, weight_q, weight_k, weight_v = low[4:]
    held = [None, None]
    held[0] = (rows, weight_q, *low[:3], gate_w)
    sums = [low[3], None]
    levels_of = [[], []]

    def step_of(half, mask):
        return over_ctx(sums[half], mask)

    def advance(**arrived):
        names = {"low": 0, "high": 1}
        fresh = added(*[(sums[names[name]], value) for name, value in arrived.items()])
        for (name, value), total in zip(arrived.items(), fresh):
            levels_of[names[name]].append(value)
            sums[names[name]] = total

    near = {}
    masks = (1, 3, 4, 12)
    low_x1 = step_of(0, masks[0])
    high = key_value(heads, dim, half_rows, (rows, weight_k, weight_v), False)
    held[1] = (rows, weight_q, *high[:3], gate_w)
    sums[1] = high[3]
    low_x1, sums[1] = lax.optimization_barrier((low_x1, sums[1]))
    advance(low=low_x1)
    low_x3, high_x1 = step_of(0, masks[1]), step_of(1, masks[0])

    def block_after(half, step, value):
        start, *others = held[half]
        start, value = lax.optimization_barrier((start, value))
        near[half, step] = near_part((start, *others), value, half, step, heads, dim)
        return value

    sums[0] = block_after(0, 0, sums[0])
    low_x3, high_x1, near[0, 0] = lax.optimization_barrier((low_x3, high_x1, near[0, 0]))
    advance(low=low_x3, high=high_x1)
    low_z1, high_x3 = step_of(0, masks[2]), step_of(1, masks[1])
    sums[0] = block_after(0, 1, sums[0])
    low_z1, high_x3, near[0, 1] = lax.optimization_barrier((low_z1, high_x3, near[0, 1]))
    advance(low=low_z1, high=high_x3)
    low_z3, high_z1 = step_of(0, masks[3]), step_of(1, masks[2])
    sums[0] = block_after(1, 0, sums[0])
    low_z3, high_z1, near[1, 0] = lax.optimization_barrier((low_z3, high_z1, near[1, 0]))
    advance(low=low_z3, high=high_z1)
    high_z3 = step_of(1, masks[3])
    levels_of[1].append(high_z3)
    levels_of[1].append(sums[0])

    def joined(*terms):
        return functools.reduce(jnp.add, [term.astype(F32) for term in terms]).astype(BF16)

    def attended(half, after):
        parts = [near[half, 0], near[half, 1]]
        return far_part(where_ctx, after, parts, gain, levels_of[half], heads, dim, level0)

    def sent(own, peer):
        return project(where_head, ring, own, peer, output_weight, peer_weight, feats)

    own_low = attended(0, sums[0])
    peer_low = over_core(own_low)
    near[1, 1] = near_part(held[1], own_low, 1, 1, heads, dim)
    sends = [sent(own_low, peer_low)]
    own_high = attended(1, sends[0][0])
    sends.append(sent(own_high, over_core(own_high)))
    results = []

    low_pair = [over_ring(sends[0][0], 1), over_ring(sends[0][1], -1)]
    high_pair = [over_ring(sends[1][0], 1), over_ring(sends[1][1], -1)]
    arrived = [low_pair, high_pair]
    for half in range(2):
        up, down, mine = sends[half][2:]
        make = lambda: relay(up, down, *arrived[half], sends[1][0])
        up, down = make()
        results.append(joined(mine, over_ring(up, 1), over_ring(down, -1)))
    return jnp.concatenate(results, axis=0)


def solution(mesh):
    placed = (
        P("ctx", None),
        P(None, None, "head"),
        P("head", None, None),
        P("head"),
        P("head", None),
    )
    return jax.shard_map(
        shards, mesh=mesh, in_specs=placed, out_specs=P("ctx", "head"), check_vma=False
    )
```

```python
import functools

import jax
import jax.numpy as jnp
from jax import lax
from jax.experimental import pallas as pl
from jax.experimental.pallas import tpu as pltpu
from jax.sharding import PartitionSpec as P

BF16 = jnp.bfloat16
F32 = jnp.float32
BLOCK = 512
CHUNK = 256
TILE = 128
KV = 28
SMALL = 4


def dot(a, b):
    return jnp.dot(a, b, preferred_element_type=F32)


def dot_nt(a, b):
    return lax.dot_general(a, b, (((1,), (1,)), ((), ())), preferred_element_type=F32)


def cost(flops, mib):
    return pl.CostEstimate(flops=flops, bytes_accessed=mib << 20, transcendentals=0)


def bits_of(number):
    return sum((number >= 2**j).astype(jnp.int32) for j in range(4))


def key_value_block(heads, dim, block, rows, wk, wv, k_out, vt_out, chunk_out, total, keys=None):
    at = slice(block * BLOCK, (block + 1) * BLOCK)
    if keys is None:
        keys = dot(rows, wk[...])
    keys = keys.astype(BF16)
    k_out[at] = keys
    values = dot(rows, wv[...]).astype(BF16)
    for head in range(heads):
        cols = slice(head * dim, (head + 1) * dim)
        turned = values[:, cols].T
        vt_out[block, cols] = turned
        sums = None if block == 0 else total[head]
        for chunk in range(2):
            inner = slice(chunk * CHUNK, (chunk + 1) * CHUNK)
            state = dot(turned[:, inner], keys[inner, cols])
            chunk_out[2 * block + chunk, head] = state.astype(BF16)
            sums = state if sums is None else sums + state
        total[head] = sums


def first_kernel(heads, dim, tok_in, w_in, k_out, vt_out, chunk_out, total_out, tok, wq, wk, wv, total, sems):
    depth = tok.shape[1]
    part = depth // 2
    blocks = k_out.shape[0] // BLOCK
    head_rows = pl.ds(0, BLOCK)
    pairs = []
    for j in range(2):
        at = pl.ds(j * part, part)
        pairs.append((w_in.at[1, at], wk.at[at]))
        pairs.append((tok_in.at[head_rows, at], tok.at[head_rows, at]))
    pairs.append((w_in.at[2], wv))
    rows = k_out.shape[0]
    for start, stop in ((BLOCK, rows), (rows, tok.shape[0])):
        at = pl.ds(start, stop - start)
        pairs.append((tok_in.at[at], tok.at[at]))
    pairs.append((w_in.at[0], wq))
    copies = [pltpu.make_async_copy(*pair, sems.at[j]) for j, pair in enumerate(pairs)]
    for copy in copies[:4]:
        copy.start()
    keys = None
    for j in range(2):
        copies[2 * j].wait()
        copies[2 * j + 1].wait()
        copies[4 + j].start()
        at = slice(j * part, (j + 1) * part)
        term = dot(tok[:BLOCK, at], wk[at])
        keys = term if keys is None else keys + term
    copies[4].wait()
    copies[6].start()
    copies[7].start()
    outs = (wk, wv, k_out, vt_out, chunk_out, total)
    key_value_block(heads, dim, 0, tok[:BLOCK], *outs, keys)
    copies[5].wait()
    for block in range(1, blocks):
        key_value_block(heads, dim, block, tok[block * BLOCK : (block + 1) * BLOCK], *outs)
    copies[6].wait()
    copies[7].wait()
    total_out[...] = total[...].astype(BF16)


def second_kernel(heads, dim, tok, wk, wv, k_out, vt_out, chunk_out, total_out, total):
    half = tok.shape[0] // 2
    for block in range(half // BLOCK):
        at = slice(half + block * BLOCK, half + (block + 1) * BLOCK)
        key_value_block(heads, dim, block, tok[at], wk, wv, k_out, vt_out, chunk_out, total)
    total_out[...] = total[...].astype(BF16)


def key_value(heads, dim, rows, args, first):
    depth = args[0].shape[1]
    width = heads * dim
    vmem = pl.BlockSpec(memory_space=pltpu.VMEM)
    shapes = [
        jax.ShapeDtypeStruct((rows, width), BF16),
        jax.ShapeDtypeStruct((rows // BLOCK, width, BLOCK), BF16),
        jax.ShapeDtypeStruct((rows // CHUNK, heads, dim, dim), BF16),
        jax.ShapeDtypeStruct((heads, dim, dim), BF16),
    ]
    scratch = [pltpu.VMEM((heads, dim, dim), F32)]
    if first:
        shapes.append(jax.ShapeDtypeStruct(args[0].shape, BF16))
        shapes += [jax.ShapeDtypeStruct((depth, width), BF16)] * 3
        scratch.append(pltpu.SemaphoreType.DMA((8,)))
    return pl.pallas_call(
        functools.partial(first_kernel if first else second_kernel, heads, dim),
        in_specs=[pl.BlockSpec(memory_space=pltpu.HBM)] * 2 if first else [vmem] * 3,
        out_specs=[vmem] * len(shapes),
        out_shape=shapes,
        scratch_shapes=scratch,
        compiler_params=pltpu.CompilerParams(vmem_limit_bytes=(KV if first else SMALL) << 20),
        cost_estimate=cost(4 * rows * depth * width, 14),
        name="key_value",
    )(*args)


def sums_kernel(*refs):
    count = len(refs) // 3
    for j in range(count):
        refs[2 * count + j][...] = (refs[2 * j][...].astype(F32) + refs[2 * j + 1][...].astype(F32)).astype(BF16)


def added(*pairs):
    vmem = pl.BlockSpec(memory_space=pltpu.VMEM)
    flat = [value for pair in pairs for value in pair]
    return pl.pallas_call(
        sums_kernel,
        in_specs=[vmem] * len(flat),
        out_specs=[vmem] * len(pairs),
        out_shape=[jax.ShapeDtypeStruct(pair[0].shape, BF16) for pair in pairs],
        compiler_params=pltpu.CompilerParams(vmem_limit_bytes=SMALL << 20),
        cost_estimate=cost(1 << 18, 1),
        name="added",
    )(*flat)


def near_kernel(
    heads, dim, half, step, tok, wq, keys, vt, states, level_w, after, near_out, q_out, coef_out, steps_ref
):
    del after
    first = half * (tok.shape[0] // 2) + step * BLOCK
    k_ref = keys.at[pl.ds(step * BLOCK, BLOCK)]
    vt_ref = vt.at[step]
    queries = dot(tok[first : first + BLOCK], wq[...]).astype(BF16)
    q_out[...] = queries
    levels = level_w.shape[0]
    count = levels * heads
    flat = level_w[...].astype(F32).reshape(count, dim)
    owner = lax.broadcasted_iota(jnp.int32, (count, heads * dim), 0) % heads
    lane_head = lax.broadcasted_iota(jnp.int32, (count, heads * dim), 1) // dim
    gate_w = jnp.where(owner == lane_head, jnp.concatenate([flat] * heads, axis=1), 0.0)
    logits = dot_nt(gate_w.astype(BF16), queries)
    gate = jnp.maximum(logits, 0.0) + jnp.log1p(jnp.exp(-jnp.abs(logits)))
    level_at = lax.broadcasted_iota(jnp.int32, logits.shape, 0) // heads
    coef_out[...] = gate * jnp.exp2(-0.5 * level_at.astype(F32))

    def row(head, level, count, at=slice(None)):
        return coef_out[pl.ds(level * heads + head, count, stride=0), :][:, at]

    lane = lax.broadcasted_iota(jnp.int32, (16, BLOCK), 1)
    group = lax.broadcasted_iota(jnp.int32, (16, BLOCK), 0)
    query_group = jnp.bitwise_and(lane, TILE - 1) // 8
    apart = bits_of(jnp.bitwise_xor(query_group, group))
    before = query_group > group
    lane8 = jnp.bitwise_and(lane[:8], 7)
    key8 = group[:8]
    near8 = bits_of(jnp.bitwise_xor(lane8, key8))
    causal8 = lane8 >= key8
    tile_group = jnp.bitwise_and(lax.broadcasted_iota(jnp.int32, (8, CHUNK), 1), TILE - 1) // 8
    for head in range(heads):
        cols = slice(head * dim, (head + 1) * dim)
        rough = jnp.zeros((16, BLOCK), F32)
        for level in range(1, 5):
            rough = jnp.where(apart == level, row(head, level + 3, 16), rough)
        steps_ref[...] = jnp.where(before, rough, 0.0)
        fine = row(head, 0, 8)
        for level in range(1, 4):
            fine = jnp.where(near8 == level, row(head, level, 8), fine)
        fine = jnp.where(causal8, fine, 0.0)
        pair = (states[0, head].astype(F32) + states[1, head].astype(F32)).astype(BF16)
        for chunk in range(2):
            at = slice(chunk * CHUNK, (chunk + 1) * CHUNK)
            query = queries[at, cols]
            left = [k_ref[at, cols]]
            if step == 1:
                left.append(pair)
            if chunk == 1:
                left.append(states[2 * step, head])
            score = dot_nt(jnp.concatenate(left, axis=0), query)
            top, bottom = [], []
            across = row(head, 8, 8, slice(chunk * CHUNK + TILE, (chunk + 1) * CHUNK))
            for j in range(16):
                weight = jnp.where(
                    tile_group == j, fine[:, at], steps_ref[pl.ds(j, 8, stride=0), :][:, at]
                )
                low = score[8 * j : 8 * j + 8]
                high = score[TILE + 8 * j : TILE + 8 * j + 8, TILE:]
                top.append(
                    jnp.concatenate([low[:, :TILE] * weight[:, :TILE], low[:, TILE:] * across], axis=1)
                )
                bottom.append(
                    jnp.concatenate([jnp.zeros((8, TILE), F32), high * weight[:, TILE:]], axis=1)
                )
            mixed = jnp.concatenate(top + bottom, axis=0).astype(BF16)
            near = dot(vt_ref[cols, at], mixed)
            wider = ([10] if step == 1 else []) + ([9] if chunk == 1 else [])
            for order, level in enumerate(wider):
                scale = jnp.concatenate([row(head, level, 8, at)] * (dim // 8), axis=0)
                near = near + scale * score[CHUNK + order * dim : CHUNK + (order + 1) * dim]
            near_out[cols, at] = near


def near_part(held, after, half, step, heads, dim):
    depth = held[0].shape[1]
    width = heads * dim
    vmem = pl.BlockSpec(memory_space=pltpu.VMEM)
    return pl.pallas_call(
        functools.partial(near_kernel, heads, dim, half, step),
        in_specs=[vmem] * 6 + [pl.BlockSpec(memory_space=pl.ANY)],
        out_specs=[vmem] * 3,
        out_shape=[
            jax.ShapeDtypeStruct((width, BLOCK), F32),
            jax.ShapeDtypeStruct((BLOCK, width), BF16),
            jax.ShapeDtypeStruct((held[5].shape[0] * heads, BLOCK), F32),
        ],
        scratch_shapes=[pltpu.VMEM((16, BLOCK), F32)],
        compiler_params=pltpu.CompilerParams(vmem_limit_bytes=SMALL << 20),
        cost_estimate=cost(4 * BLOCK * depth * width, 14),
        name="near_part",
    )(*held, after)


def far_kernel(heads, dim, level0, count, half, device, after, gain, *refs):
    del after
    bits = [(device[0] >> level) & 1 for level in range(4)]
    flags = [(bit if half == 0 else 1 - bit).astype(F32) for bit in bits]
    blocks = (len(refs) - count - 2) // 3
    states, (out, gains) = refs[3 * blocks : -2], refs[-2:]
    for head in range(heads):
        cols = slice(head * dim, (head + 1) * dim)
        gains[cols] = jnp.broadcast_to(gain[:, cols], (dim, dim)).T
    for block in range(blocks):
        near, q_ref, coef_ref = refs[3 * block : 3 * block + 3]
        for head in range(heads):
            cols = slice(head * dim, (head + 1) * dim)
            far = jnp.concatenate([state[head] for state in states], axis=0)
            for chunk in range(2):
                at = slice(chunk * CHUNK, (chunk + 1) * CHUNK)
                terms = dot_nt(far, q_ref[at, cols])
                acc = near[cols, at]
                for level in range(count):
                    lane = (level0 + level) * heads + head
                    scale = coef_ref[pl.ds(lane, 8, stride=0), :][:, at]
                    if level < 4:
                        scale = scale * flags[level]
                    scale = jnp.concatenate([scale] * (dim // 8), axis=0)
                    acc = acc + scale * terms[level * dim : (level + 1) * dim]
                mean = jnp.mean(acc * acc, axis=0, keepdims=True)
                both = jnp.concatenate([gains[cols], gains[cols]], axis=1)
                rows = slice(block * BLOCK + chunk * CHUNK, block * BLOCK + (chunk + 1) * CHUNK)
                out[rows, cols] = (acc * lax.rsqrt(mean + 1e-06) * both).astype(BF16).T


def far_part(device, after, near, gain, states, heads, dim, level0):
    rows = len(near) * BLOCK
    width = heads * dim
    count = len(states)
    blocks = [part for block in near for part in block]
    vmem = pl.BlockSpec(memory_space=pltpu.VMEM)
    return pl.pallas_call(
        functools.partial(far_kernel, heads, dim, level0, count, count - 4),
        in_specs=[pl.BlockSpec(memory_space=pltpu.SMEM), pl.BlockSpec(memory_space=pl.ANY)]
        + [vmem] * (1 + len(blocks) + count),
        out_specs=vmem,
        out_shape=jax.ShapeDtypeStruct((rows, width), BF16),
        scratch_shapes=[pltpu.VMEM((width, dim), F32)],
        compiler_params=pltpu.CompilerParams(vmem_limit_bytes=SMALL << 20),
        cost_estimate=cost(2 * rows * dim * width * count, 5),
        name="far_part",
    )(device, after, gain, *blocks, *states)


def project_kernel(feats, ring, group, own, peer, w_own, w_peer, *outs):
    block = own.shape[0] // 2
    for order, shift in enumerate((2, 1, ring - 1, 0)):
        slot = 2 * (((group[0] >> 1) + shift) % ring) + (group[0] & 1)
        at = pl.ds(pl.multiple_of(slot * feats, feats), feats)
        for part in range(2):
            rows = slice(part * block, (part + 1) * block)
            total = dot(own[rows], w_own[:, at]) + dot(peer[rows], w_peer[:, at])
            out = outs[2 * order + part]
            out[...] = total.astype(out.dtype)


def project(group, ring, own, peer, w_own, w_peer, feats):
    rows, width = own.shape
    vmem = pl.BlockSpec(memory_space=pltpu.VMEM)
    size = (rows // 2, feats)
    return pl.pallas_call(
        functools.partial(project_kernel, feats, ring),
        in_specs=[pl.BlockSpec(memory_space=pltpu.SMEM)] + [vmem] * 4,
        out_specs=[vmem] * 8,
        out_shape=[jax.ShapeDtypeStruct(size, BF16)] * 6 + [jax.ShapeDtypeStruct(size, F32)] * 2,
        compiler_params=pltpu.CompilerParams(vmem_limit_bytes=12 << 20),
        cost_estimate=cost(16 * rows * width * feats, 4),
        name="project",
    )(group, own, peer, w_own, w_peer)


def relay_kernel(up_in, down_in, from_down, from_up, *refs):
    up, down = refs[-2:]
    block = from_down.shape[0]
    up[:block] = (up_in[...].astype(F32) + from_down[...].astype(F32)).astype(BF16)
    down[:block] = (down_in[...].astype(F32) + from_up[...].astype(F32)).astype(BF16)
    for extra, out in zip(refs[:-2], (up, down)):
        out[block:] = extra[...]


def relay(up, down, from_down, from_up, *extra):
    rows, feats = up.shape
    vmem = pl.BlockSpec(memory_space=pltpu.VMEM)
    total = 2 * rows if extra else rows
    return pl.pallas_call(
        relay_kernel,
        in_specs=[vmem] * (4 + len(extra)),
        out_specs=[vmem] * 2,
        out_shape=[jax.ShapeDtypeStruct((total, feats), BF16)] * 2,
        compiler_params=pltpu.CompilerParams(vmem_limit_bytes=SMALL << 20),
        cost_estimate=cost(1 << 18, 1),
        name="relay",
    )(up, down, from_down, from_up, *extra)


def final_kernel(half, parts, *refs):
    out, stage, sems = refs[-3:]
    block = stage.shape[1]
    copies = []
    for part in range(2):
        own, first, second = refs[3 * part : 3 * part + 3]
        (at1, at2) = parts[part]
        total = own[...] + first[at1 : at1 + block].astype(F32) + second[at2 : at2 + block].astype(F32)
        stage[part] = total.astype(BF16)
        rows = pl.ds((2 * half + part) * block, block)
        copies.append(pltpu.make_async_copy(stage.at[part], out.at[rows], sems.at[part]))
        copies[-1].start()
    for copy in copies:
        copy.wait()


def final(half, terms, parts, base):
    block, feats = terms[0].shape
    vmem = pl.BlockSpec(memory_space=pltpu.VMEM)
    hbm = pl.BlockSpec(memory_space=pltpu.HBM)
    args, specs, alias = list(terms), [vmem] * 6, {}
    if base is not None:
        args, specs, alias = args + [base], specs + [hbm], {6: 0}
    return pl.pallas_call(
        functools.partial(final_kernel, half, parts),
        in_specs=specs,
        out_specs=hbm,
        out_shape=jax.ShapeDtypeStruct((4 * block, feats), BF16),
        scratch_shapes=[pltpu.VMEM((2, block, feats), BF16), pltpu.SemaphoreType.DMA((2,))],
        input_output_aliases=alias,
        compiler_params=pltpu.CompilerParams(vmem_limit_bytes=SMALL << 20),
        cost_estimate=cost(1 << 18, 2),
        name="final",
    )(*args)


def shards(tokens, project_weight, level_weight, norm_gain, output_weight):
    heads, dim, _ = level_weight.shape
    half_rows = tokens.shape[0] // 2
    ctx_count = lax.axis_size("ctx")
    head_count = lax.axis_size("head")
    feats = output_weight.shape[1] // head_count
    device = lax.axis_index("ctx")
    group = lax.axis_index("head")
    ring = head_count // 2
    level0 = half_rows.bit_length()

    def over_core(value):
        return lax.ppermute(value, "head", [(i, i ^ 1) for i in range(head_count)])

    def over_ring(value, shift):
        return lax.ppermute(
            value, "head", [(i, (i + 2 * shift) % head_count) for i in range(head_count)]
        )

    weights = jnp.transpose(project_weight, (1, 0, 2))
    peer_weight = over_core(output_weight)
    gate_w = jnp.transpose(level_weight, (2, 0, 1))
    gain = norm_gain[None]
    tokens, where_ctx, where_head = lax.optimization_barrier(
        (tokens, device.reshape(1), group.reshape(1))
    )

    def over_ctx(value, mask):
        return lax.ppermute(value, "ctx", [(i, i ^ mask) for i in range(ctx_count)])

    weights = pltpu.with_memory_space_constraint(weights, pltpu.HBM)
    tokens = pltpu.with_memory_space_constraint(tokens, pltpu.HBM)
    low = key_value(heads, dim, half_rows, (tokens, weights), True)
    rows, weight_q, weight_k, weight_v = low[4:]
    held = [None, None]
    held[0] = (rows, weight_q, *low[:3], gate_w)
    sums = [low[3], None]
    levels_of = [[], []]

    def step_of(half, mask):
        return over_ctx(sums[half], mask)

    def advance(**arrived):
        names = {"low": 0, "high": 1}
        fresh = added(*[(sums[names[name]], value) for name, value in arrived.items()])
        for (name, value), total in zip(arrived.items(), fresh):
            levels_of[names[name]].append(value)
            sums[names[name]] = total

    near = {}
    masks = (1, 3, 4, 12)
    low_x1 = step_of(0, masks[0])
    high = key_value(heads, dim, half_rows, (rows, weight_k, weight_v), False)
    held[1] = (rows, weight_q, *high[:3], gate_w)
    sums[1] = high[3]
    low_x1, sums[1] = lax.optimization_barrier((low_x1, sums[1]))
    advance(low=low_x1)
    low_x3, high_x1 = step_of(0, masks[1]), step_of(1, masks[0])

    def block_after(half, step, value):
        start, *others = held[half]
        start, value = lax.optimization_barrier((start, value))
        near[half, step] = near_part((start, *others), value, half, step, heads, dim)
        return value

    sums[0] = block_after(0, 0, sums[0])
    low_x3, high_x1, near[0, 0] = lax.optimization_barrier((low_x3, high_x1, near[0, 0]))
    advance(low=low_x3, high=high_x1)
    low_z1, high_x3 = step_of(0, masks[2]), step_of(1, masks[1])
    sums[0] = block_after(0, 1, sums[0])
    low_z1, high_x3, near[0, 1] = lax.optimization_barrier((low_z1, high_x3, near[0, 1]))
    advance(low=low_z1, high=high_x3)
    low_z3, high_z1 = step_of(0, masks[3]), step_of(1, masks[2])
    sums[0] = block_after(1, 0, sums[0])
    low_z3, high_z1, near[1, 0] = lax.optimization_barrier((low_z3, high_z1, near[1, 0]))
    advance(low=low_z3, high=high_z1)
    high_z3 = step_of(1, masks[3])
    levels_of[1].append(high_z3)
    levels_of[1].append(sums[0])

    def attended(half, after):
        parts = [near[half, 0], near[half, 1]]
        return far_part(where_ctx, after, parts, gain, levels_of[half], heads, dim, level0)

    def sent(own, peer):
        return project(where_head, ring, own, peer, output_weight, peer_weight, feats)

    def sent_over(value, shift):
        return over_ring(value, shift)

    own_low = attended(0, sums[0])
    peer_low = over_core(own_low)
    near[1, 1] = near_part(held[1], own_low, 1, 1, heads, dim)
    top, bottom, up_a, up_b, down_a, down_b, low_a, low_b = sent(own_low, peer_low)
    low_pair = [sent_over(top, 1), sent_over(bottom, -1)]
    own_high = attended(1, top)
    low_up_b, low_down_a = sent_over(up_b, 1), sent_over(down_a, -1)
    peer_high = over_core(own_high)
    top, bottom, high_up_a, high_up_b, high_down_a, high_down_b, high_a, high_b = sent(own_high, peer_high)
    high_pair = [sent_over(top, 1), sent_over(bottom, -1)]
    up_mix, down_mix = relay(up_a, down_b, *low_pair, high_up_b, high_down_a)
    up_mix, down_mix = sent_over(up_mix, 1), sent_over(down_mix, -1)
    up_last, down_last = relay(high_up_a, high_down_b, *high_pair)
    up_last, down_last = over_ring(up_last, 1), over_ring(down_last, -1)
    block = half_rows // 2
    low_terms = (low_a, up_mix, low_down_a, low_b, low_up_b, down_mix)
    result = final(0, low_terms, ((0, 0), (0, 0)), None)
    high_terms = (high_a, up_last, down_mix, high_b, up_mix, down_last)
    return final(1, high_terms, ((0, block), (block, 0)), result)


def solution(mesh):
    placed = (
        P("ctx", None),
        P(None, None, "head"),
        P("head", None, None),
        P("head"),
        P("head", None),
    )
    return jax.shard_map(
        shards, mesh=mesh, in_specs=placed, out_specs=P("ctx", "head"), check_vma=False
    )
```

```python
import functools

import jax
import jax.numpy as jnp
from jax import lax
from jax.experimental import pallas as pl
from jax.experimental.pallas import tpu as pltpu
from jax.sharding import PartitionSpec as P

BF16 = jnp.bfloat16
F32 = jnp.float32
BLOCK = 512
CHUNK = 256
TILE = 128
KV = 28
SMALL = 4


def dot(a, b):
    return jnp.dot(a, b, preferred_element_type=F32)


def dot_nt(a, b):
    return lax.dot_general(a, b, (((1,), (1,)), ((), ())), preferred_element_type=F32)


def cost(flops, mib):
    return pl.CostEstimate(flops=flops, bytes_accessed=mib << 20, transcendentals=0)


def bits_of(number):
    return sum((number >= 2**j).astype(jnp.int32) for j in range(4))


def key_value_block(heads, dim, block, rows, wk, wv, k_out, vt_out, chunk_out, total, keys=None):
    at = slice(block * BLOCK, (block + 1) * BLOCK)
    if keys is None:
        keys = dot(rows, wk[...])
    keys = keys.astype(BF16)
    k_out[at] = keys
    values = dot(rows, wv[...]).astype(BF16)
    for head in range(heads):
        cols = slice(head * dim, (head + 1) * dim)
        turned = values[:, cols].T
        vt_out[block, cols] = turned
        sums = None if block == 0 else total[head]
        for chunk in range(2):
            inner = slice(chunk * CHUNK, (chunk + 1) * CHUNK)
            state = dot(turned[:, inner], keys[inner, cols])
            chunk_out[2 * block + chunk, head] = state.astype(BF16)
            sums = state if sums is None else sums + state
        total[head] = sums


def first_kernel(heads, dim, tok_in, w_in, k_out, vt_out, chunk_out, total_out, tok, wq, wk, wv, total, sems):
    depth = tok.shape[1]
    part = depth // 2
    blocks = k_out.shape[0] // BLOCK
    head_rows = pl.ds(0, BLOCK)
    pairs = []
    for j in range(2):
        at = pl.ds(j * part, part)
        pairs.append((w_in.at[1, at], wk.at[at]))
        pairs.append((tok_in.at[head_rows, at], tok.at[head_rows, at]))
    pairs.append((w_in.at[2], wv))
    rows = k_out.shape[0]
    for start, stop in ((BLOCK, rows), (rows, tok.shape[0])):
        at = pl.ds(start, stop - start)
        pairs.append((tok_in.at[at], tok.at[at]))
    pairs.append((w_in.at[0], wq))
    copies = [pltpu.make_async_copy(*pair, sems.at[j]) for j, pair in enumerate(pairs)]
    for copy in copies[:4]:
        copy.start()
    keys = None
    for j in range(2):
        copies[2 * j].wait()
        copies[2 * j + 1].wait()
        copies[4 + j].start()
        at = slice(j * part, (j + 1) * part)
        term = dot(tok[:BLOCK, at], wk[at])
        keys = term if keys is None else keys + term
    copies[4].wait()
    copies[6].start()
    copies[7].start()
    outs = (wk, wv, k_out, vt_out, chunk_out, total)
    key_value_block(heads, dim, 0, tok[:BLOCK], *outs, keys)
    copies[5].wait()
    for block in range(1, blocks):
        key_value_block(heads, dim, block, tok[block * BLOCK : (block + 1) * BLOCK], *outs)
    copies[6].wait()
    copies[7].wait()
    total_out[...] = total[...].astype(BF16)


def second_kernel(heads, dim, tok, wk, wv, k_out, vt_out, chunk_out, total_out, total):
    half = tok.shape[0] // 2
    for block in range(half // BLOCK):
        at = slice(half + block * BLOCK, half + (block + 1) * BLOCK)
        key_value_block(heads, dim, block, tok[at], wk, wv, k_out, vt_out, chunk_out, total)
    total_out[...] = total[...].astype(BF16)


def key_value(heads, dim, rows, args, first):
    depth = args[0].shape[1]
    width = heads * dim
    vmem = pl.BlockSpec(memory_space=pltpu.VMEM)
    shapes = [
        jax.ShapeDtypeStruct((rows, width), BF16),
        jax.ShapeDtypeStruct((rows // BLOCK, width, BLOCK), BF16),
        jax.ShapeDtypeStruct((rows // CHUNK, heads, dim, dim), BF16),
        jax.ShapeDtypeStruct((heads, dim, dim), BF16),
    ]
    scratch = [pltpu.VMEM((heads, dim, dim), F32)]
    if first:
        shapes.append(jax.ShapeDtypeStruct(args[0].shape, BF16))
        shapes += [jax.ShapeDtypeStruct((depth, width), BF16)] * 3
        scratch.append(pltpu.SemaphoreType.DMA((8,)))
    return pl.pallas_call(
        functools.partial(first_kernel if first else second_kernel, heads, dim),
        in_specs=[pl.BlockSpec(memory_space=pltpu.HBM)] * 2 if first else [vmem] * 3,
        out_specs=[vmem] * len(shapes),
        out_shape=shapes,
        scratch_shapes=scratch,
        compiler_params=pltpu.CompilerParams(vmem_limit_bytes=(KV if first else SMALL) << 20),
        cost_estimate=cost(4 * rows * depth * width, 14),
        name="key_value",
    )(*args)


def sums_kernel(*refs):
    count = len(refs) // 3
    for j in range(count):
        refs[2 * count + j][...] = (refs[2 * j][...].astype(F32) + refs[2 * j + 1][...].astype(F32)).astype(BF16)


def added(*pairs):
    vmem = pl.BlockSpec(memory_space=pltpu.VMEM)
    flat = [value for pair in pairs for value in pair]
    return pl.pallas_call(
        sums_kernel,
        in_specs=[vmem] * len(flat),
        out_specs=[vmem] * len(pairs),
        out_shape=[jax.ShapeDtypeStruct(pair[0].shape, BF16) for pair in pairs],
        compiler_params=pltpu.CompilerParams(vmem_limit_bytes=SMALL << 20),
        cost_estimate=cost(1 << 18, 1),
        name="added",
    )(*flat)


def near_kernel(
    heads, dim, half, step, tok, wq, keys, vt, states, level_w, after, near_out, q_out, coef_out, steps_ref
):
    del after
    first = half * (tok.shape[0] // 2) + step * BLOCK
    k_ref = keys.at[pl.ds(step * BLOCK, BLOCK)]
    vt_ref = vt.at[step]
    queries = dot(tok[first : first + BLOCK], wq[...]).astype(BF16)
    q_out[...] = queries
    levels = level_w.shape[0]
    count = levels * heads
    flat = level_w[...].astype(F32).reshape(count, dim)
    owner = lax.broadcasted_iota(jnp.int32, (count, heads * dim), 0) % heads
    lane_head = lax.broadcasted_iota(jnp.int32, (count, heads * dim), 1) // dim
    gate_w = jnp.where(owner == lane_head, jnp.concatenate([flat] * heads, axis=1), 0.0)
    logits = dot_nt(gate_w.astype(BF16), queries)
    gate = jnp.maximum(logits, 0.0) + jnp.log1p(jnp.exp(-jnp.abs(logits)))
    level_at = lax.broadcasted_iota(jnp.int32, logits.shape, 0) // heads
    coef_out[...] = gate * jnp.exp2(-0.5 * level_at.astype(F32))

    def row(head, level, count, at=slice(None)):
        return coef_out[pl.ds(level * heads + head, count, stride=0), :][:, at]

    lane = lax.broadcasted_iota(jnp.int32, (16, BLOCK), 1)
    group = lax.broadcasted_iota(jnp.int32, (16, BLOCK), 0)
    query_group = jnp.bitwise_and(lane, TILE - 1) // 8
    apart = bits_of(jnp.bitwise_xor(query_group, group))
    before = query_group > group
    lane8 = jnp.bitwise_and(lane[:8], 7)
    key8 = group[:8]
    near8 = bits_of(jnp.bitwise_xor(lane8, key8))
    causal8 = lane8 >= key8
    tile_group = jnp.bitwise_and(lax.broadcasted_iota(jnp.int32, (8, CHUNK), 1), TILE - 1) // 8

    def weights_of(head):
        rough = jnp.zeros((16, BLOCK), F32)
        for level in range(1, 5):
            rough = jnp.where(apart == level, row(head, level + 3, 16), rough)
        steps_ref[head] = jnp.where(before, rough, 0.0)
        fine = row(head, 0, 8)
        for level in range(1, 4):
            fine = jnp.where(near8 == level, row(head, level, 8), fine)
        return jnp.where(causal8, fine, 0.0)

    def scores_of(head, chunk):
        cols = slice(head * dim, (head + 1) * dim)
        at = slice(chunk * CHUNK, (chunk + 1) * CHUNK)
        left = [k_ref[at, cols]]
        if step == 1:
            left.append((states[0, head].astype(F32) + states[1, head].astype(F32)).astype(BF16))
        if chunk == 1:
            left.append(states[2 * step, head])
        return dot_nt(jnp.concatenate(left, axis=0), queries[at, cols])

    def mixed_of(head, chunk, score, fine):
        at = slice(chunk * CHUNK, (chunk + 1) * CHUNK)
        top, bottom = [], []
        across = row(head, 8, 8, slice(chunk * CHUNK + TILE, (chunk + 1) * CHUNK))
        for j in range(16):
            weight = jnp.where(
                tile_group == j, fine[:, at], steps_ref.at[head][pl.ds(j, 8, stride=0), :][:, at]
            )
            low = score[8 * j : 8 * j + 8]
            high = score[TILE + 8 * j : TILE + 8 * j + 8, TILE:]
            top.append(
                jnp.concatenate([low[:, :TILE] * weight[:, :TILE], low[:, TILE:] * across], axis=1)
            )
            bottom.append(
                jnp.concatenate([jnp.zeros((8, TILE), F32), high * weight[:, TILE:]], axis=1)
            )
        return jnp.concatenate(top + bottom, axis=0).astype(BF16)

    def finish(head, chunk, score, mixed):
        cols = slice(head * dim, (head + 1) * dim)
        at = slice(chunk * CHUNK, (chunk + 1) * CHUNK)
        near = dot(vt_ref[cols, at], mixed)
        wider = ([10] if step == 1 else []) + ([9] if chunk == 1 else [])
        for order, level in enumerate(wider):
            scale = jnp.concatenate([row(head, level, 8, at)] * (dim // 8), axis=0)
            near = near + scale * score[CHUNK + order * dim : CHUNK + (order + 1) * dim]
        near_out[cols, at] = near

    for first_head in range(0, heads, 2):
        pair = (first_head, first_head + 1)
        fines = {head: weights_of(head) for head in pair}
        units = [(head, chunk) for head in pair for chunk in range(2)]
        scores = [scores_of(*unit) for unit in units]
        mixes = [mixed_of(*unit, score, fines[unit[0]]) for unit, score in zip(units, scores)]
        for unit, score, mixed in zip(units, scores, mixes):
            finish(*unit, score, mixed)


def near_part(held, after, half, step, heads, dim):
    depth = held[0].shape[1]
    width = heads * dim
    vmem = pl.BlockSpec(memory_space=pltpu.VMEM)
    return pl.pallas_call(
        functools.partial(near_kernel, heads, dim, half, step),
        in_specs=[vmem] * 6 + [pl.BlockSpec(memory_space=pl.ANY)],
        out_specs=[vmem] * 3,
        out_shape=[
            jax.ShapeDtypeStruct((width, BLOCK), F32),
            jax.ShapeDtypeStruct((BLOCK, width), BF16),
            jax.ShapeDtypeStruct((held[5].shape[0] * heads, BLOCK), F32),
        ],
        scratch_shapes=[pltpu.VMEM((heads, 16, BLOCK), F32)],
        compiler_params=pltpu.CompilerParams(vmem_limit_bytes=SMALL << 20),
        cost_estimate=cost(4 * BLOCK * depth * width, 14),
        name="near_part",
    )(*held, after)


def far_kernel(heads, dim, level0, count, half, device, after, gain, *refs):
    del after
    bits = [(device[0] >> level) & 1 for level in range(4)]
    flags = [(bit if half == 0 else 1 - bit).astype(F32) for bit in bits]
    blocks = (len(refs) - count - 2) // 3
    states, (out, gains) = refs[3 * blocks : -2], refs[-2:]
    for head in range(heads):
        cols = slice(head * dim, (head + 1) * dim)
        gains[cols] = jnp.broadcast_to(gain[:, cols], (dim, dim)).T
    for block in range(blocks):
        near, q_ref, coef_ref = refs[3 * block : 3 * block + 3]
        for head in range(heads):
            cols = slice(head * dim, (head + 1) * dim)
            far = jnp.concatenate([state[head] for state in states], axis=0)
            for chunk in range(2):
                at = slice(chunk * CHUNK, (chunk + 1) * CHUNK)
                terms = dot_nt(far, q_ref[at, cols])
                acc = near[cols, at]
                for level in range(count):
                    lane = (level0 + level) * heads + head
                    scale = coef_ref[pl.ds(lane, 8, stride=0), :][:, at]
                    if level < 4:
                        scale = scale * flags[level]
                    scale = jnp.concatenate([scale] * (dim // 8), axis=0)
                    acc = acc + scale * terms[level * dim : (level + 1) * dim]
                mean = jnp.mean(acc * acc, axis=0, keepdims=True)
                both = jnp.concatenate([gains[cols], gains[cols]], axis=1)
                rows = slice(block * BLOCK + chunk * CHUNK, block * BLOCK + (chunk + 1) * CHUNK)
                out[rows, cols] = (acc * lax.rsqrt(mean + 1e-06) * both).astype(BF16).T


def far_part(device, after, near, gain, states, heads, dim, level0):
    rows = len(near) * BLOCK
    width = heads * dim
    count = len(states)
    blocks = [part for block in near for part in block]
    vmem = pl.BlockSpec(memory_space=pltpu.VMEM)
    return pl.pallas_call(
        functools.partial(far_kernel, heads, dim, level0, count, count - 4),
        in_specs=[pl.BlockSpec(memory_space=pltpu.SMEM), pl.BlockSpec(memory_space=pl.ANY)]
        + [vmem] * (1 + len(blocks) + count),
        out_specs=vmem,
        out_shape=jax.ShapeDtypeStruct((rows, width), BF16),
        scratch_shapes=[pltpu.VMEM((width, dim), F32)],
        compiler_params=pltpu.CompilerParams(vmem_limit_bytes=SMALL << 20),
        cost_estimate=cost(2 * rows * dim * width * count, 5),
        name="far_part",
    )(device, after, gain, *blocks, *states)


def project_kernel(feats, ring, shifts, group, own, peer, w_own, w_peer, *outs):
    block = own.shape[0] // 2
    for order, shift in enumerate(shifts):
        slot = 2 * (((group[0] >> 1) + shift) % ring) + (group[0] & 1)
        at = pl.ds(pl.multiple_of(slot * feats, feats), feats)
        for part in range(2):
            rows = slice(part * block, (part + 1) * block)
            total = dot(own[rows], w_own[:, at]) + dot(peer[rows], w_peer[:, at])
            out = outs[2 * order + part]
            out[...] = total.astype(out.dtype)


def project(group, ring, own, peer, w_own, w_peer, feats, shifts):
    rows, width = own.shape
    vmem = pl.BlockSpec(memory_space=pltpu.VMEM)
    size = (rows // 2, feats)
    return pl.pallas_call(
        functools.partial(project_kernel, feats, ring, shifts),
        in_specs=[pl.BlockSpec(memory_space=pltpu.SMEM)] + [vmem] * 4,
        out_specs=[vmem] * (2 * len(shifts)),
        out_shape=[
            jax.ShapeDtypeStruct(size, BF16 if shift else F32) for shift in shifts for _ in range(2)
        ],
        compiler_params=pltpu.CompilerParams(vmem_limit_bytes=12 << 20),
        cost_estimate=cost(4 * rows * width * feats * len(shifts), 4),
        name="project",
    )(group, own, peer, w_own, w_peer)


def relay_kernel(up_in, down_in, from_down, from_up, *refs):
    up, down = refs[-2:]
    block = from_down.shape[0]
    up[:block] = (up_in[...].astype(F32) + from_down[...].astype(F32)).astype(BF16)
    down[:block] = (down_in[...].astype(F32) + from_up[...].astype(F32)).astype(BF16)
    for extra, out in zip(refs[:-2], (up, down)):
        out[block:] = extra[...]


def relay(up, down, from_down, from_up, *extra):
    rows, feats = up.shape
    vmem = pl.BlockSpec(memory_space=pltpu.VMEM)
    total = 2 * rows if extra else rows
    return pl.pallas_call(
        relay_kernel,
        in_specs=[vmem] * (4 + len(extra)),
        out_specs=[vmem] * 2,
        out_shape=[jax.ShapeDtypeStruct((total, feats), BF16)] * 2,
        compiler_params=pltpu.CompilerParams(vmem_limit_bytes=SMALL << 20),
        cost_estimate=cost(1 << 18, 1),
        name="relay",
    )(up, down, from_down, from_up, *extra)


def final_kernel(half, parts, *refs):
    out, stage, sems = refs[-3:]
    block = stage.shape[1]
    copies = []
    for part in range(2):
        own, first, second = refs[3 * part : 3 * part + 3]
        (at1, at2) = parts[part]
        total = own[...] + first[at1 : at1 + block].astype(F32) + second[at2 : at2 + block].astype(F32)
        stage[part] = total.astype(BF16)
        rows = pl.ds((2 * half + part) * block, block)
        copies.append(pltpu.make_async_copy(stage.at[part], out.at[rows], sems.at[part]))
        copies[-1].start()
    for copy in copies:
        copy.wait()


def final(half, terms, parts, base):
    block, feats = terms[0].shape
    vmem = pl.BlockSpec(memory_space=pltpu.VMEM)
    hbm = pl.BlockSpec(memory_space=pltpu.HBM)
    args, specs, alias = list(terms), [vmem] * 6, {}
    if base is not None:
        args, specs, alias = args + [base], specs + [hbm], {6: 0}
    return pl.pallas_call(
        functools.partial(final_kernel, half, parts),
        in_specs=specs,
        out_specs=hbm,
        out_shape=jax.ShapeDtypeStruct((4 * block, feats), BF16),
        scratch_shapes=[pltpu.VMEM((2, block, feats), BF16), pltpu.SemaphoreType.DMA((2,))],
        input_output_aliases=alias,
        compiler_params=pltpu.CompilerParams(vmem_limit_bytes=SMALL << 20),
        cost_estimate=cost(1 << 18, 2),
        name="final",
    )(*args)


def shards(tokens, project_weight, level_weight, norm_gain, output_weight):
    heads, dim, _ = level_weight.shape
    half_rows = tokens.shape[0] // 2
    ctx_count = lax.axis_size("ctx")
    head_count = lax.axis_size("head")
    feats = output_weight.shape[1] // head_count
    device = lax.axis_index("ctx")
    group = lax.axis_index("head")
    ring = head_count // 2
    level0 = half_rows.bit_length()

    def over_core(value):
        return lax.ppermute(value, "head", [(i, i ^ 1) for i in range(head_count)])

    def over_ring(value, shift):
        return lax.ppermute(
            value, "head", [(i, (i + 2 * shift) % head_count) for i in range(head_count)]
        )

    weights = jnp.transpose(project_weight, (1, 0, 2))
    peer_weight = over_core(output_weight)
    gate_w = jnp.transpose(level_weight, (2, 0, 1))
    gain = norm_gain[None]
    tokens, where_ctx, where_head = lax.optimization_barrier(
        (tokens, device.reshape(1), group.reshape(1))
    )

    def over_ctx(value, mask):
        return lax.ppermute(value, "ctx", [(i, i ^ mask) for i in range(ctx_count)])

    weights = pltpu.with_memory_space_constraint(weights, pltpu.HBM)
    tokens = pltpu.with_memory_space_constraint(tokens, pltpu.HBM)
    low = key_value(heads, dim, half_rows, (tokens, weights), True)
    rows, weight_q, weight_k, weight_v = low[4:]
    held = [None, None]
    held[0] = (rows, weight_q, *low[:3], gate_w)
    sums = [low[3], None]
    levels_of = [[], []]

    def step_of(half, mask):
        return over_ctx(sums[half], mask)

    def advance(half, arrived):
        levels_of[half].append(arrived)
        sums[half] = added((sums[half], arrived))[0]

    near = {}
    masks = (1, 3, 4, 12)
    low = step_of(0, masks[0])
    high = key_value(heads, dim, half_rows, (rows, weight_k, weight_v), False)
    held[1] = (rows, weight_q, *high[:3], gate_w)
    sums[1] = high[3]
    low, sums[1] = lax.optimization_barrier((low, sums[1]))
    high = step_of(1, masks[0])
    advance(0, low)
    low = step_of(0, masks[1])
    for index, (half, step) in enumerate(((0, 0), (0, 1), (1, 0))):
        after = sums[0] if index == 0 else sums[1]
        make = lambda: near_part(held[half], after, half, step, heads, dim)
        near[half, step] = make()
        low, near[half, step] = lax.optimization_barrier((low, near[half, step]))
        if index == 2:
            break
        advance(0, low)
        low = step_of(0, masks[index + 2])
        advance(1, high)
        high = step_of(1, masks[index + 1])
    levels_of[0].append(low)

    def attended(half, after):
        parts = [near[half, 0], near[half, 1]]
        return far_part(where_ctx, after, parts, gain, levels_of[half], heads, dim, level0)

    def sent(own, peer, *shifts):
        return project(where_head, ring, own, peer, output_weight, peer_weight, feats, shifts)

    def sent_over(value, shift):
        return over_ring(value, shift)

    own_low = attended(0, near[1, 0][2])
    peer_low = over_core(own_low)
    advance(1, high)
    levels_of[1].append(step_of(1, masks[3]))
    levels_of[1].append(added((sums[0], low))[0])
    near[1, 1] = near_part(held[1], own_low, 1, 1, heads, dim)
    top, bottom = sent(own_low, peer_low, 2)
    low_pair = [sent_over(top, 1), sent_over(bottom, -1)]
    own_high = attended(1, top)
    up_a, up_b, down_a, down_b, low_a, low_b = sent(own_low, peer_low, 1, ring - 1, 0)
    low_up_b, low_down_a = sent_over(up_b, 1), sent_over(down_a, -1)
    peer_high = over_core(own_high)
    top, bottom = sent(own_high, peer_high, 2)
    high_pair = [sent_over(top, 1), sent_over(bottom, -1)]
    high_up_a, high_up_b, high_down_a, high_down_b, high_a, high_b = sent(own_high, peer_high, 1, ring - 1, 0)
    up_mix, down_mix = relay(up_a, down_b, *low_pair, high_up_b, high_down_a)
    up_mix, down_mix = sent_over(up_mix, 1), sent_over(down_mix, -1)
    up_last, down_last = relay(high_up_a, high_down_b, *high_pair)
    up_last, down_last = over_ring(up_last, 1), over_ring(down_last, -1)
    block = half_rows // 2
    low_terms = (low_a, up_mix, low_down_a, low_b, low_up_b, down_mix)
    result = final(0, low_terms, ((0, 0), (0, 0)), None)
    high_terms = (high_a, up_last, down_mix, high_b, up_mix, down_last)
    return final(1, high_terms, ((0, block), (block, 0)), result)


def solution(mesh):
    placed = (
        P("ctx", None),
        P(None, None, "head"),
        P("head", None, None),
        P("head"),
        P("head", None),
    )
    return jax.shard_map(
        shards, mesh=mesh, in_specs=placed, out_specs=P("ctx", "head"), check_vma=False
    )
```

```python
import functools

import jax
import jax.numpy as jnp
from jax import lax
from jax.experimental import pallas as pl
from jax.experimental.pallas import tpu as pltpu
from jax.sharding import PartitionSpec as P

BF16 = jnp.bfloat16
F32 = jnp.float32
BLOCK = 512
CHUNK = 256
TILE = 128
KV = 28
SMALL = 4


def dot(a, b):
    return jnp.dot(a, b, preferred_element_type=F32)


def dot_nt(a, b):
    return lax.dot_general(a, b, (((1,), (1,)), ((), ())), preferred_element_type=F32)


def cost(flops, mib):
    return pl.CostEstimate(flops=flops, bytes_accessed=mib << 20, transcendentals=0)


def bits_of(number):
    return sum((number >= 2**j).astype(jnp.int32) for j in range(4))


def key_value_block(
    heads, dim, block, rows, wk, wv, k_out, vt_out, chunk_out, total, keys=None, values=None
):
    at = slice(block * BLOCK, (block + 1) * BLOCK)
    if keys is None:
        keys = dot(rows, wk[...])
    keys = keys.astype(BF16)
    k_out[at] = keys
    if values is None:
        values = dot(rows, wv[...])
    values = values.astype(BF16)
    for head in range(heads):
        cols = slice(head * dim, (head + 1) * dim)
        turned = values[:, cols].T
        vt_out[block, cols] = turned
        sums = None if block == 0 else total[head]
        for chunk in range(2):
            inner = slice(chunk * CHUNK, (chunk + 1) * CHUNK)
            state = dot(turned[:, inner], keys[inner, cols])
            chunk_out[2 * block + chunk, head] = state.astype(BF16)
            sums = state if sums is None else sums + state
        total[head] = sums


def first_kernel(heads, dim, tok_in, w_in, k_out, vt_out, chunk_out, total_out, tok, wq, wk, wv, total, sems):
    depth = tok.shape[1]
    parts = 4
    part = depth // parts
    rows = k_out.shape[0]
    blocks = rows // BLOCK
    opening = pl.ds(0, BLOCK)
    pairs = []
    for j in range(parts):
        at = pl.ds(j * part, part)
        pairs.append((w_in.at[1, at], wk.at[at]))
        pairs.append((tok_in.at[opening, at], tok.at[opening, at]))
    for j in range(parts):
        at = pl.ds(j * part, part)
        pairs.append((w_in.at[2, at], wv.at[at]))
    for start, stop in ((BLOCK, rows), (rows, tok.shape[0])):
        at = pl.ds(start, stop - start)
        pairs.append((tok_in.at[at], tok.at[at]))
    pairs.append((w_in.at[0], wq))
    copies = [pltpu.make_async_copy(*pair, sems.at[j]) for j, pair in enumerate(pairs)]
    later = copies[2 * parts :]
    for copy in copies[: 2 * parts]:
        copy.start()
    keys = values = None
    for j in range(parts):
        copies[2 * j].wait()
        copies[2 * j + 1].wait()
        later[j].start()
        at = slice(j * part, (j + 1) * part)
        term = dot(tok[:BLOCK, at], wk[at])
        keys = term if keys is None else keys + term
    later[parts].start()
    for j in range(parts):
        later[j].wait()
        at = slice(j * part, (j + 1) * part)
        term = dot(tok[:BLOCK, at], wv[at])
        values = term if values is None else values + term
    later[parts + 1].start()
    later[parts + 2].start()
    outs = (wk, wv, k_out, vt_out, chunk_out, total)
    key_value_block(heads, dim, 0, tok[:BLOCK], *outs, keys, values)
    later[parts].wait()
    for block in range(1, blocks):
        key_value_block(heads, dim, block, tok[block * BLOCK : (block + 1) * BLOCK], *outs)
    later[parts + 1].wait()
    later[parts + 2].wait()
    total_out[...] = total[...].astype(BF16)


def second_kernel(heads, dim, tok, wk, wv, k_out, vt_out, chunk_out, total_out, total):
    half = tok.shape[0] // 2
    for block in range(half // BLOCK):
        at = slice(half + block * BLOCK, half + (block + 1) * BLOCK)
        key_value_block(heads, dim, block, tok[at], wk, wv, k_out, vt_out, chunk_out, total)
    total_out[...] = total[...].astype(BF16)


def key_value(heads, dim, rows, args, first):
    depth = args[0].shape[1]
    width = heads * dim
    vmem = pl.BlockSpec(memory_space=pltpu.VMEM)
    shapes = [
        jax.ShapeDtypeStruct((rows, width), BF16),
        jax.ShapeDtypeStruct((rows // BLOCK, width, BLOCK), BF16),
        jax.ShapeDtypeStruct((rows // CHUNK, heads, dim, dim), BF16),
        jax.ShapeDtypeStruct((heads, dim, dim), BF16),
    ]
    scratch = [pltpu.VMEM((heads, dim, dim), F32)]
    if first:
        shapes.append(jax.ShapeDtypeStruct(args[0].shape, BF16))
        shapes += [jax.ShapeDtypeStruct((depth, width), BF16)] * 3
        scratch.append(pltpu.SemaphoreType.DMA((15,)))
    return pl.pallas_call(
        functools.partial(first_kernel if first else second_kernel, heads, dim),
        in_specs=[pl.BlockSpec(memory_space=pltpu.HBM)] * 2 if first else [vmem] * 3,
        out_specs=[vmem] * len(shapes),
        out_shape=shapes,
        scratch_shapes=scratch,
        compiler_params=pltpu.CompilerParams(vmem_limit_bytes=(KV if first else SMALL) << 20),
        cost_estimate=cost(4 * rows * depth * width, 14),
        name="key_value",
    )(*args)


def sums_kernel(*refs):
    count = len(refs) // 3
    for j in range(count):
        refs[2 * count + j][...] = (refs[2 * j][...].astype(F32) + refs[2 * j + 1][...].astype(F32)).astype(BF16)


def added(*pairs):
    vmem = pl.BlockSpec(memory_space=pltpu.VMEM)
    flat = [value for pair in pairs for value in pair]
    return pl.pallas_call(
        sums_kernel,
        in_specs=[vmem] * len(flat),
        out_specs=[vmem] * len(pairs),
        out_shape=[jax.ShapeDtypeStruct(pair[0].shape, BF16) for pair in pairs],
        compiler_params=pltpu.CompilerParams(vmem_limit_bytes=SMALL << 20),
        cost_estimate=cost(1 << 18, 1),
        name="added",
    )(*flat)


def near_kernel(
    heads, dim, half, step, tok, wq, keys, vt, states, level_w, after, near_out, q_out, coef_out, steps_ref
):
    del after
    first = half * (tok.shape[0] // 2) + step * BLOCK
    k_ref = keys.at[pl.ds(step * BLOCK, BLOCK)]
    vt_ref = vt.at[step]
    queries = dot(tok[first : first + BLOCK], wq[...]).astype(BF16)
    q_out[...] = queries
    levels = level_w.shape[0]
    count = levels * heads
    flat = level_w[...].astype(F32).reshape(count, dim)
    owner = lax.broadcasted_iota(jnp.int32, (count, heads * dim), 0) % heads
    lane_head = lax.broadcasted_iota(jnp.int32, (count, heads * dim), 1) // dim
    gate_w = jnp.where(owner == lane_head, jnp.concatenate([flat] * heads, axis=1), 0.0)
    logits = dot_nt(gate_w.astype(BF16), queries)
    gate = jnp.maximum(logits, 0.0) + jnp.log1p(jnp.exp(-jnp.abs(logits)))
    level_at = lax.broadcasted_iota(jnp.int32, logits.shape, 0) // heads
    coef_out[...] = gate * jnp.exp2(-0.5 * level_at.astype(F32))

    def row(head, level, count, at=slice(None)):
        return coef_out[pl.ds(level * heads + head, count, stride=0), :][:, at]

    lane = lax.broadcasted_iota(jnp.int32, (16, BLOCK), 1)
    group = lax.broadcasted_iota(jnp.int32, (16, BLOCK), 0)
    query_group = jnp.bitwise_and(lane, TILE - 1) // 8
    apart = bits_of(jnp.bitwise_xor(query_group, group))
    before = query_group > group
    lane8 = jnp.bitwise_and(lane[:8], 7)
    key8 = group[:8]
    near8 = bits_of(jnp.bitwise_xor(lane8, key8))
    causal8 = lane8 >= key8
    tile_group = jnp.bitwise_and(lax.broadcasted_iota(jnp.int32, (8, CHUNK), 1), TILE - 1) // 8

    def weights_of(head):
        rough = jnp.zeros((16, BLOCK), F32)
        for level in range(1, 5):
            rough = jnp.where(apart == level, row(head, level + 3, 16), rough)
        steps_ref[head] = jnp.where(before, rough, 0.0)
        fine = row(head, 0, 8)
        for level in range(1, 4):
            fine = jnp.where(near8 == level, row(head, level, 8), fine)
        return jnp.where(causal8, fine, 0.0)

    def scores_of(head, chunk):
        cols = slice(head * dim, (head + 1) * dim)
        at = slice(chunk * CHUNK, (chunk + 1) * CHUNK)
        left = [k_ref[at, cols]]
        if step == 1:
            left.append((states[0, head].astype(F32) + states[1, head].astype(F32)).astype(BF16))
        if chunk == 1:
            left.append(states[2 * step, head])
        return dot_nt(jnp.concatenate(left, axis=0), queries[at, cols])

    def mixed_of(head, chunk, score, fine):
        at = slice(chunk * CHUNK, (chunk + 1) * CHUNK)
        top, bottom = [], []
        across = row(head, 8, 8, slice(chunk * CHUNK + TILE, (chunk + 1) * CHUNK))
        for j in range(16):
            weight = jnp.where(
                tile_group == j, fine[:, at], steps_ref.at[head][pl.ds(j, 8, stride=0), :][:, at]
            )
            low = score[8 * j : 8 * j + 8]
            high = score[TILE + 8 * j : TILE + 8 * j + 8, TILE:]
            top.append(
                jnp.concatenate([low[:, :TILE] * weight[:, :TILE], low[:, TILE:] * across], axis=1)
            )
            bottom.append(
                jnp.concatenate([jnp.zeros((8, TILE), F32), high * weight[:, TILE:]], axis=1)
            )
        return jnp.concatenate(top + bottom, axis=0).astype(BF16)

    def finish(head, chunk, score, mixed):
        cols = slice(head * dim, (head + 1) * dim)
        at = slice(chunk * CHUNK, (chunk + 1) * CHUNK)
        near = dot(vt_ref[cols, at], mixed)
        wider = ([10] if step == 1 else []) + ([9] if chunk == 1 else [])
        for order, level in enumerate(wider):
            scale = jnp.concatenate([row(head, level, 8, at)] * (dim // 8), axis=0)
            near = near + scale * score[CHUNK + order * dim : CHUNK + (order + 1) * dim]
        near_out[cols, at] = near

    for first_head in range(0, heads, 2):
        pair = (first_head, first_head + 1)
        fines = {head: weights_of(head) for head in pair}
        units = [(head, chunk) for head in pair for chunk in range(2)]
        scores = [scores_of(*unit) for unit in units]
        mixes = [mixed_of(*unit, score, fines[unit[0]]) for unit, score in zip(units, scores)]
        for unit, score, mixed in zip(units, scores, mixes):
            finish(*unit, score, mixed)


def near_part(held, after, half, step, heads, dim):
    depth = held[0].shape[1]
    width = heads * dim
    vmem = pl.BlockSpec(memory_space=pltpu.VMEM)
    return pl.pallas_call(
        functools.partial(near_kernel, heads, dim, half, step),
        in_specs=[vmem] * 6 + [pl.BlockSpec(memory_space=pl.ANY)],
        out_specs=[vmem] * 3,
        out_shape=[
            jax.ShapeDtypeStruct((width, BLOCK), F32),
            jax.ShapeDtypeStruct((BLOCK, width), BF16),
            jax.ShapeDtypeStruct((held[5].shape[0] * heads, BLOCK), F32),
        ],
        scratch_shapes=[pltpu.VMEM((heads, 16, BLOCK), F32)],
        compiler_params=pltpu.CompilerParams(vmem_limit_bytes=SMALL << 20),
        cost_estimate=cost(4 * BLOCK * depth * width, 14),
        name="near_part",
    )(*held, after)


def far_kernel(heads, dim, level0, count, half, device, after, gain, *refs):
    del after
    bits = [(device[0] >> level) & 1 for level in range(4)]
    flags = [(bit if half == 0 else 1 - bit).astype(F32) for bit in bits]
    blocks = (len(refs) - count - 2) // 3
    states, (out, gains) = refs[3 * blocks : -2], refs[-2:]
    for head in range(heads):
        cols = slice(head * dim, (head + 1) * dim)
        gains[cols] = jnp.broadcast_to(gain[:, cols], (dim, dim)).T
    for block in range(blocks):
        near, q_ref, coef_ref = refs[3 * block : 3 * block + 3]
        for head in range(heads):
            cols = slice(head * dim, (head + 1) * dim)
            far = jnp.concatenate([state[head] for state in states], axis=0)
            for chunk in range(2):
                at = slice(chunk * CHUNK, (chunk + 1) * CHUNK)
                terms = dot_nt(far, q_ref[at, cols])
                acc = near[cols, at]
                for level in range(count):
                    lane = (level0 + level) * heads + head
                    scale = coef_ref[pl.ds(lane, 8, stride=0), :][:, at]
                    if level < 4:
                        scale = scale * flags[level]
                    scale = jnp.concatenate([scale] * (dim // 8), axis=0)
                    acc = acc + scale * terms[level * dim : (level + 1) * dim]
                mean = jnp.mean(acc * acc, axis=0, keepdims=True)
                both = jnp.concatenate([gains[cols], gains[cols]], axis=1)
                rows = slice(block * BLOCK + chunk * CHUNK, block * BLOCK + (chunk + 1) * CHUNK)
                out[rows, cols] = (acc * lax.rsqrt(mean + 1e-06) * both).astype(BF16).T


def far_part(device, after, near, gain, states, heads, dim, level0):
    rows = len(near) * BLOCK
    width = heads * dim
    count = len(states)
    blocks = [part for block in near for part in block]
    vmem = pl.BlockSpec(memory_space=pltpu.VMEM)
    return pl.pallas_call(
        functools.partial(far_kernel, heads, dim, level0, count, count - 4),
        in_specs=[pl.BlockSpec(memory_space=pltpu.SMEM), pl.BlockSpec(memory_space=pl.ANY)]
        + [vmem] * (1 + len(blocks) + count),
        out_specs=vmem,
        out_shape=jax.ShapeDtypeStruct((rows, width), BF16),
        scratch_shapes=[pltpu.VMEM((width, dim), F32)],
        compiler_params=pltpu.CompilerParams(vmem_limit_bytes=SMALL << 20),
        cost_estimate=cost(2 * rows * dim * width * count, 5),
        name="far_part",
    )(device, after, gain, *blocks, *states)


def project_kernel(feats, ring, shifts, group, own, peer, w_own, w_peer, *outs):
    block = own.shape[0] // 2
    for order, shift in enumerate(shifts):
        slot = 2 * (((group[0] >> 1) + shift) % ring) + (group[0] & 1)
        at = pl.ds(pl.multiple_of(slot * feats, feats), feats)
        for part in range(2):
            rows = slice(part * block, (part + 1) * block)
            total = dot(own[rows], w_own[:, at]) + dot(peer[rows], w_peer[:, at])
            out = outs[2 * order + part]
            out[...] = total.astype(out.dtype)


def project(group, ring, own, peer, w_own, w_peer, feats, shifts):
    rows, width = own.shape
    vmem = pl.BlockSpec(memory_space=pltpu.VMEM)
    size = (rows // 2, feats)
    return pl.pallas_call(
        functools.partial(project_kernel, feats, ring, shifts),
        in_specs=[pl.BlockSpec(memory_space=pltpu.SMEM)] + [vmem] * 4,
        out_specs=[vmem] * (2 * len(shifts)),
        out_shape=[
            jax.ShapeDtypeStruct(size, BF16 if shift else F32) for shift in shifts for _ in range(2)
        ],
        compiler_params=pltpu.CompilerParams(vmem_limit_bytes=12 << 20),
        cost_estimate=cost(4 * rows * width * feats * len(shifts), 4),
        name="project",
    )(group, own, peer, w_own, w_peer)


def relay_kernel(up_in, down_in, from_down, from_up, *refs):
    up, down = refs[-2:]
    block = from_down.shape[0]
    up[:block] = (up_in[...].astype(F32) + from_down[...].astype(F32)).astype(BF16)
    down[:block] = (down_in[...].astype(F32) + from_up[...].astype(F32)).astype(BF16)
    for extra, out in zip(refs[:-2], (up, down)):
        out[block:] = extra[...]


def relay(up, down, from_down, from_up, *extra):
    rows, feats = up.shape
    vmem = pl.BlockSpec(memory_space=pltpu.VMEM)
    total = 2 * rows if extra else rows
    return pl.pallas_call(
        relay_kernel,
        in_specs=[vmem] * (4 + len(extra)),
        out_specs=[vmem] * 2,
        out_shape=[jax.ShapeDtypeStruct((total, feats), BF16)] * 2,
        compiler_params=pltpu.CompilerParams(vmem_limit_bytes=SMALL << 20),
        cost_estimate=cost(1 << 18, 1),
        name="relay",
    )(up, down, from_down, from_up, *extra)


def final_kernel(half, parts, *refs):
    out, stage, sems = refs[-3:]
    block = stage.shape[1]
    copies = []
    for part in range(2):
        own, first, second = refs[3 * part : 3 * part + 3]
        (at1, at2) = parts[part]
        total = own[...] + first[at1 : at1 + block].astype(F32) + second[at2 : at2 + block].astype(F32)
        stage[part] = total.astype(BF16)
        rows = pl.ds((2 * half + part) * block, block)
        copies.append(pltpu.make_async_copy(stage.at[part], out.at[rows], sems.at[part]))
        copies[-1].start()
    for copy in copies:
        copy.wait()


def final(half, terms, parts, base):
    block, feats = terms[0].shape
    vmem = pl.BlockSpec(memory_space=pltpu.VMEM)
    hbm = pl.BlockSpec(memory_space=pltpu.HBM)
    args, specs, alias = list(terms), [vmem] * 6, {}
    if base is not None:
        args, specs, alias = args + [base], specs + [hbm], {6: 0}
    return pl.pallas_call(
        functools.partial(final_kernel, half, parts),
        in_specs=specs,
        out_specs=hbm,
        out_shape=jax.ShapeDtypeStruct((4 * block, feats), BF16),
        scratch_shapes=[pltpu.VMEM((2, block, feats), BF16), pltpu.SemaphoreType.DMA((2,))],
        input_output_aliases=alias,
        compiler_params=pltpu.CompilerParams(vmem_limit_bytes=SMALL << 20),
        cost_estimate=cost(1 << 18, 2),
        name="final",
    )(*args)


def shards(tokens, project_weight, level_weight, norm_gain, output_weight):
    heads, dim, _ = level_weight.shape
    half_rows = tokens.shape[0] // 2
    ctx_count = lax.axis_size("ctx")
    head_count = lax.axis_size("head")
    feats = output_weight.shape[1] // head_count
    device = lax.axis_index("ctx")
    group = lax.axis_index("head")
    ring = head_count // 2
    level0 = half_rows.bit_length()

    def over_core(value):
        return lax.ppermute(value, "head", [(i, i ^ 1) for i in range(head_count)])

    def over_ring(value, shift):
        return lax.ppermute(
            value, "head", [(i, (i + 2 * shift) % head_count) for i in range(head_count)]
        )

    weights = jnp.transpose(project_weight, (1, 0, 2))
    peer_weight = over_core(output_weight)
    gate_w = jnp.transpose(level_weight, (2, 0, 1))
    gain = norm_gain[None]
    tokens, where_ctx, where_head = lax.optimization_barrier(
        (tokens, device.reshape(1), group.reshape(1))
    )

    def over_ctx(value, mask):
        return lax.ppermute(value, "ctx", [(i, i ^ mask) for i in range(ctx_count)])

    weights = pltpu.with_memory_space_constraint(weights, pltpu.HBM)
    tokens = pltpu.with_memory_space_constraint(tokens, pltpu.HBM)
    low = key_value(heads, dim, half_rows, (tokens, weights), True)
    rows, weight_q, weight_k, weight_v = low[4:]
    held = [None, None]
    held[0] = (rows, weight_q, *low[:3], gate_w)
    sums = [low[3], None]
    levels_of = [[], []]

    def step_of(half, mask):
        return over_ctx(sums[half], mask)

    def advance(half, arrived):
        levels_of[half].append(arrived)
        sums[half] = added((sums[half], arrived))[0]

    near = {}
    masks = (1, 3, 4, 12)
    low = step_of(0, masks[0])
    high = key_value(heads, dim, half_rows, (rows, weight_k, weight_v), False)
    held[1] = (rows, weight_q, *high[:3], gate_w)
    sums[1] = high[3]
    low, sums[1] = lax.optimization_barrier((low, sums[1]))
    high = step_of(1, masks[0])
    advance(0, low)
    low = step_of(0, masks[1])
    for index, (half, step) in enumerate(((0, 0), (0, 1), (1, 0))):
        after = sums[0] if index == 0 else sums[1]
        make = lambda: near_part(held[half], after, half, step, heads, dim)
        near[half, step] = make()
        low, near[half, step] = lax.optimization_barrier((low, near[half, step]))
        if index == 2:
            break
        advance(0, low)
        low = step_of(0, masks[index + 2])
        advance(1, high)
        high = step_of(1, masks[index + 1])
    levels_of[0].append(low)

    def attended(half, after):
        parts = [near[half, 0], near[half, 1]]
        return far_part(where_ctx, after, parts, gain, levels_of[half], heads, dim, level0)

    def sent(own, peer, *shifts):
        return project(where_head, ring, own, peer, output_weight, peer_weight, feats, shifts)

    def sent_over(value, shift):
        return over_ring(value, shift)

    own_low = attended(0, near[1, 0][2])
    peer_low = over_core(own_low)
    advance(1, high)
    levels_of[1].append(step_of(1, masks[3]))
    levels_of[1].append(added((sums[0], low))[0])
    near[1, 1] = near_part(held[1], own_low, 1, 1, heads, dim)
    top, bottom = sent(own_low, peer_low, 2)
    low_pair = [sent_over(top, 1), sent_over(bottom, -1)]
    own_high = attended(1, top)
    up_a, up_b, down_a, down_b, low_a, low_b = sent(own_low, peer_low, 1, ring - 1, 0)
    low_up_b, low_down_a = sent_over(up_b, 1), sent_over(down_a, -1)
    peer_high = over_core(own_high)
    top, bottom = sent(own_high, peer_high, 2)
    high_pair = [sent_over(top, 1), sent_over(bottom, -1)]
    high_up_a, high_up_b, high_down_a, high_down_b, high_a, high_b = sent(own_high, peer_high, 1, ring - 1, 0)
    up_mix, down_mix = relay(up_a, down_b, *low_pair, high_up_b, high_down_a)
    up_mix, down_mix = sent_over(up_mix, 1), sent_over(down_mix, -1)
    up_last, down_last = relay(high_up_a, high_down_b, *high_pair)
    up_last, down_last = over_ring(up_last, 1), over_ring(down_last, -1)
    block = half_rows // 2
    low_terms = (low_a, up_mix, low_down_a, low_b, low_up_b, down_mix)
    result = final(0, low_terms, ((0, 0), (0, 0)), None)
    high_terms = (high_a, up_last, down_mix, high_b, up_mix, down_last)
    return final(1, high_terms, ((0, block), (block, 0)), result)


def solution(mesh):
    placed = (
        P("ctx", None),
        P(None, None, "head"),
        P("head", None, None),
        P("head"),
        P("head", None),
    )
    return jax.shard_map(
        shards, mesh=mesh, in_specs=placed, out_specs=P("ctx", "head"), check_vma=False
    )
```
